32 devices in a mesh: gx: 4 (over x, core), gy: 8 (over z, y).
Axes of the slice: x: 2, y: 2, z: 4, core: 2. Of those that a mesh axis runs over, the one named last changes fastest.
Arguments:
- fields: float32 [5, 192, 18432], P(None, 'gx', 'gy'), may hold values from -6 to 6
- winds: float32 [3, 192, 18432], P(None, 'gx', 'gy'), may hold values from -0.1 to 0.1
- diffusion: float32 [192, 18432], P('gx', 'gy'), may hold values from 0.02 to 0.06
- droplets: float32 [16384, 12, 128], P(('gx', 'gy')), may hold values from -3 to 3, as said below
- cells: int32 [16384, 128], P(('gx', 'gy')), may hold values from 0 to 110591, as said below
- balance_list: int32 [16384], P(('gx', 'gy')), may hold values from -1 to 8191, as said below
Outputs:
- fields_out: float32 [5, 192, 18432], P(None, 'gx', 'gy')
- droplets_out: float32 [8192, 12, 128], P(('gx', 'gy'))
The draws below stay inside these ranges and needn't reach their ends.
Inputs may be any that keep to these rules, and one draw needn't show every extreme that they name: `droplets`: Rows: radius in 0.3 to 2, solute term in 0.003 to 0.03, weight in 0.5 to 2, positions and aerosol fractions in 0 to 1, velocities in -3 to 3. `cells`: A cell is (x * 48 + y) * 48 + z in the home tile. All 128 droplets of a block lie in one column (x, y), and within a block the cell never falls. `balance_list`: each home's used entries come first; every value from 0 to 8191 appears exactly once; at most 16 entries of one home name one owner, and some home uses all 512 entries.
All inputs are finite; a program needn't handle non-finite values.
Results may differ from the reference program's by a relative error of at most 0.00011.
Values sent between devices are 32-bit elements; how exact they have to be, the bound alone decides.
A program may use at most 128 MiB of HBM per device.

```python
import math
import jax
import jax.numpy as jnp

CX = 48
CY = 48
NZ = 48
BLOCK = 128
OWN_BLK = 256
SUBSTEPS = 4
HOME_CAP = 512
NX = 192
NY = 384
N_GY = 8
DEVICES = 32


def draw_droplets(key, part):
    key_list = jax.random.split(jax.random.fold_in(key, 3), 6)
    shape_one = (DEVICES * HOME_CAP, 1, BLOCK)
    shape_three = (DEVICES * HOME_CAP, 3, BLOCK)
    radius = jnp.exp(jax.random.uniform(key_list[0], shape_one, jnp.float32, math.log(0.3), math.log(2.0)))
    solute = jnp.exp(jax.random.uniform(key_list[1], shape_one, jnp.float32, math.log(0.003), math.log(0.03)))
    weight = jnp.exp(jax.random.uniform(key_list[2], shape_one, jnp.float32, math.log(0.5), math.log(2.0)))
    velocity = jnp.clip(jax.random.normal(key_list[4], shape_three, jnp.float32), -3.0, 3.0)
    position = jax.random.uniform(key_list[3], shape_three, jnp.float32, 0.0, 1.0)
    aerosol = jax.random.uniform(key_list[5], shape_three, jnp.float32, 0.0, 1.0)
    radius = jnp.clip(radius, 0.3, 2.0)
    solute = jnp.clip(solute, 0.003, 0.03)
    weight = jnp.clip(weight, 0.5, 2.0)
    return jnp.concatenate([radius, solute, weight, position, velocity, aerosol], axis=1).astype(jnp.float32)


def draw_cells(key, part):
    key_list = jax.random.split(jax.random.fold_in(key, 5), 2)
    column_count = CX * CY
    raw_columns = jax.random.randint(key_list[0], (DEVICES, HOME_CAP), 0, column_count)
    raw_columns = raw_columns.at[:, 0].set(0).at[:, -1].set(column_count - 1)
    columns = jnp.sort(raw_columns, axis=1).reshape(DEVICES * HOME_CAP, 1)
    raw_levels = jax.random.randint(key_list[1], (DEVICES * HOME_CAP, BLOCK), 0, NZ)
    raw_levels = raw_levels.at[:, 0].set(0).at[:, -1].set(NZ - 1)
    levels = jnp.sort(raw_levels, axis=1)
    return (columns * NZ + levels).astype(jnp.int32)


def draw_balance_list(key, part):
    key_list = jax.random.split(jax.random.fold_in(key, 7), 3)
    pair_count = DEVICES // 2
    extra = jax.random.randint(key_list[0], (pair_count,), 0, OWN_BLK + 1)
    extra = extra.at[0].set(OWN_BLK)
    ranked = jnp.stack([OWN_BLK + extra, OWN_BLK - extra], axis=1).reshape(-1)
    home_order = jax.random.permutation(key_list[1], DEVICES)
    counts = jnp.zeros((DEVICES,), jnp.int32).at[home_order].set(ranked.astype(jnp.int32))
    starts = jnp.cumsum(counts) - counts
    slot_index = jnp.arange(HOME_CAP, dtype=jnp.int32)
    dealt = starts[:, None] + slot_index[None, :]
    live = slot_index[None, :] < counts[:, None]
    owner_order = jax.random.permutation(key_list[2], DEVICES).astype(jnp.int32)
    target = owner_order[dealt % DEVICES] * OWN_BLK + dealt // DEVICES
    return jnp.where(live, target, -1).reshape(-1).astype(jnp.int32)


def steps_of(own_key, extent, cuts, least, high):
    loudness, own = 1.0, jax.random.fold_in(own_key, 6)
    for dim, parts in cuts:
        steps = jnp.exp(jax.random.uniform(jax.random.fold_in(own, dim), (parts,), jnp.float32, least / len(cuts), high / len(cuts)))
        loudness = loudness * jnp.repeat(steps, extent[dim] // parts).reshape([-1 if axis == dim else 1 for axis in range(len(extent))])
    return loudness


def scatter_about(stream_key, dims, deviation, bound, cuts=(), kind=jnp.bfloat16):
    result = jax.random.normal(stream_key, dims, jnp.float32) * deviation
    if len(cuts) > 0:
        result = steps_of(stream_key, dims, cuts, -0.22, 0.18) * result
    return jnp.clip(result, min=-bound, max=bound).astype(kind)


def setup_inputs(seed: int = 0) -> dict:
    key_of = jax.random.split(jax.random.key(seed), 7)
    return {
        "fields": scatter_about(key_of[0], (5, NX, NY * NZ), 1.0, 6.0, ((1, 4), (2, 8)), jnp.float32),
        "winds": jnp.clip(jax.random.uniform(key_of[1], (3, NX, NY * NZ), jnp.float32, -0.1, 0.1) * steps_of(key_of[1], (3, NX, NY * NZ), ((1, 4), (2, 8)), -0.4, 0.0), -0.1, 0.1),
        "diffusion": jnp.clip(0.02 + 0.04 * jax.random.uniform(key_of[2], (NX, NY * NZ), jnp.float32) ** steps_of(key_of[2], (NX, NY * NZ), ((0, 4), (1, 8)), -0.2, 0.2), 0.02, 0.06),
        "droplets": draw_droplets(jax.random.fold_in(key_of[6], 71), 0),
        "cells": draw_cells(jax.random.fold_in(key_of[6], 71), 0),
        "balance_list": draw_balance_list(jax.random.fold_in(key_of[6], 71), 0),
    }


def face_flux(low_side, high_side, courant_low, courant_high, diff_low, diff_high):
    courant = 0.5 * (courant_low + courant_high)
    diffuse = 0.5 * (diff_low + diff_high)
    return jnp.maximum(courant, 0.0) * low_side + jnp.minimum(courant, 0.0) * high_side - diffuse * (high_side - low_side)

def cell_forcing(theta_cell, vapour_cell):
    supersat = vapour_cell - 0.5 * jnp.tanh(theta_cell)
    growth_rate = 1.0 / (1.0 + 0.1 * theta_cell * theta_cell)
    return (supersat, growth_rate)

def grow(attributes, supersat, growth_rate):
    radius_start = attributes[:, 0]
    solute = attributes[:, 1]
    weight = attributes[:, 2]
    square = radius_start * radius_start
    for substep in range(SUBSTEPS):
        radius = jnp.sqrt(square)
        square = jnp.maximum(square + 0.05 * growth_rate * (supersat - 0.02 / radius + solute / (radius * radius * radius)), 0.04)
    radius = jnp.sqrt(square)
    droplet_mass = weight * (radius * square - radius_start * radius_start * radius_start)
    position = attributes[:, 3:6] + 0.1 * attributes[:, 6:9]
    updated = jnp.concatenate([radius[:, None], attributes[:, 1:3], position, attributes[:, 6:12]], axis=1)
    return (updated, droplet_mass)

def ref_step(state, wind_grid, diff_grid):
    change = jnp.zeros_like(state)
    for axis in range(2):
        ahead = jnp.roll(state, -1, axis + 1)
        courant_here = wind_grid[axis]
        courant_ahead = jnp.roll(courant_here, -1, axis)
        diff_ahead = jnp.roll(diff_grid, -1, axis)
        flux = face_flux(state, ahead, courant_here, courant_ahead, diff_grid, diff_ahead)
        change = change + (flux - jnp.roll(flux, 1, axis + 1))
    flux_z = face_flux(state[..., :-1], state[..., 1:], wind_grid[2][..., :-1], wind_grid[2][..., 1:], diff_grid[..., :-1], diff_grid[..., 1:])
    flux_z = jnp.pad(flux_z, ((0, 0), (0, 0), (0, 0), (1, 1)))
    change = change + (flux_z[..., 1:] - flux_z[..., :-1])
    return state - change

def reference(fields, winds, diffusion, droplets, cells, balance_list):
    grid_shape = (NX, NY, NZ)
    state = fields.reshape((5,) + grid_shape)
    wind_grid = winds.reshape((3,) + grid_shape)
    diff_grid = diffusion.reshape(grid_shape)
    block_count = droplets.shape[0]
    home_tile = jnp.arange(block_count, dtype=jnp.int32) // HOME_CAP
    tile_x = (home_tile // N_GY)[:, None]
    tile_y = (home_tile % N_GY)[:, None]
    local_x = cells // (CY * NZ)
    remain = cells % (CY * NZ)
    local_y = remain // NZ
    local_z = remain % NZ
    global_cell = ((tile_x * CX + local_x) * NY + tile_y * CY + local_y) * NZ + local_z
    global_cell = global_cell.astype(jnp.int32)
    theta_flat = fields[0].reshape(-1)
    vapour_flat = fields[1].reshape(-1)
    supersat, growth_rate = cell_forcing(theta_flat[global_cell], vapour_flat[global_cell])
    updated, grown_mass = grow(droplets, supersat, growth_rate)
    live = balance_list >= 0
    droplet_mass = jnp.where(live[:, None], grown_mass, 0.0)
    condensed = jax.ops.segment_sum(droplet_mass.reshape(-1), global_cell.reshape(-1), num_segments=NX * NY * NZ)
    condensed = condensed.reshape(NX, NY * NZ)
    target = jnp.where(live, balance_list, DEVICES * OWN_BLK).astype(jnp.int32)
    droplets_out = jnp.zeros((DEVICES * OWN_BLK, 12, BLOCK), jnp.float32).at[target].set(updated, mode='drop')
    for substep in range(2):
        state = ref_step(state, wind_grid, diff_grid)
    advanced = state.reshape(5, NX, NY * NZ)
    theta_out = advanced[0] + 0.25 * condensed
    vapour_out = advanced[1] - 0.1 * condensed
    fields_out = jnp.concatenate([theta_out[None], vapour_out[None], advanced[2:5]], axis=0)
    return (fields_out, droplets_out)
```

```python
import jax
import jax.numpy as jnp
from jax import lax
from jax.experimental import pallas as pl
from jax.experimental.pallas import tpu as pltpu
from jax.sharding import PartitionSpec as P

NZ = 48
OWN_BLK = 256
SUBSTEPS = 4
LANES = 128
ROW0 = 16
VMEM = pl.BlockSpec(memory_space=pltpu.VMEM)
SMEM = pl.BlockSpec(memory_space=pltpu.SMEM)
LIMIT = 56 * 1024 * 1024


def params():
    return pltpu.CompilerParams(vmem_limit_bytes=LIMIT)


def cost(bytes_accessed, flops):
    return pl.CostEstimate(flops=flops, bytes_accessed=bytes_accessed, transcendentals=0)


def send_kernel(home_cap, send_cap, rows, base_ref, live_ref, drops_ref, out_ref):
    def body(b, carry):
        block = drops_ref[pl.ds(home_cap + b, rows, stride=home_cap), :]
        out_ref[pl.ds(base_ref[b], rows, stride=send_cap), :] = block
        return carry

    lax.fori_loop(0, live_ref[0], body, 0)


def send_rows(base, live_count, planes, home_cap, send_cap):
    rows = planes.shape[0] // home_cap - 1
    return pl.pallas_call(
        lambda *refs: send_kernel(home_cap, send_cap, rows, *refs),
        out_shape=jax.ShapeDtypeStruct((rows * home_cap, LANES), jnp.float32),
        in_specs=[SMEM, SMEM, VMEM],
        out_specs=VMEM,
        compiler_params=params(),
        cost_estimate=cost(6 << 20, 1 << 20),
        name="send_rows",
    )(base, live_count, planes)


def grow_kernel(
    home_cap,
    column_ref,
    position_ref,
    live_ref,
    table_ref,
    level_ref,
    drops_ref,
    cond_ref,
    sent_ref,
    picked,
    radius_out,
    mass,
):
    live_count = live_ref[0]

    def fetch(g, carry):
        for i in range(8):
            b = g * 8 + i
            picked[pl.ds(b, 1), :] = table_ref[pl.ds(column_ref[b], 1), :]
        return carry

    lax.fori_loop(0, home_cap // 8, fetch, 0)

    def one(g, carry):
        at = pl.multiple_of(g * 8, 8)
        rows = pl.ds(at, 8)
        level = level_ref[rows, :]
        pair = picked[rows, :]
        theta = jnp.take_along_axis(pair, level, axis=1)
        vapour = jnp.take_along_axis(pair, level + 64, axis=1)
        supersat = vapour - 0.5 * jnp.tanh(theta)
        growth_rate = 1.0 / (1.0 + 0.1 * theta * theta)
        start = drops_ref[rows, :]
        solute = drops_ref[pl.ds(home_cap + at, 8), :]
        weight = drops_ref[pl.ds(2 * home_cap + at, 8), :]
        square = start * start
        for _ in range(SUBSTEPS):
            radius = jnp.sqrt(square)
            square = jnp.maximum(
                square
                + 0.05
                * growth_rate
                * (supersat - 0.02 / radius + solute / (radius * radius * radius)),
                0.04,
            )
        radius = jnp.sqrt(square)
        radius_out[rows, :] = radius
        grown = weight * (radius * square - start * start * start)
        block = at + lax.broadcasted_iota(jnp.int32, (8, LANES), 0)
        mass[rows, :] = jnp.where(block < live_count, grown, 0.0)
        return carry

    lax.fori_loop(0, home_cap // 8, one, 0)

    def send(b, carry):
        sent_ref[pl.ds(position_ref[b], 1), :] = radius_out[pl.ds(b, 1), :]
        return carry

    lax.fori_loop(0, live_count, send, 0)
    row = lax.broadcasted_iota(jnp.int32, (LANES, LANES), 0)
    column = lax.broadcasted_iota(jnp.int32, (LANES, LANES), 1)
    upper = (row <= column).astype(jnp.float32)
    mass[...] = jnp.dot(
        mass[...], upper, precision=lax.Precision.HIGHEST, preferred_element_type=jnp.float32
    )
    cond_ref[...] = jnp.zeros_like(cond_ref)
    lane = lax.broadcasted_iota(jnp.int32, (8, LANES), 1)

    def sums(g, carry):
        rows = pl.ds(pl.multiple_of(g * 8, 8), 8)
        level = level_ref[rows, :]
        count = jnp.zeros((8, LANES), jnp.int32)
        step = LANES
        while step >= 1:
            probe = jnp.minimum(count + (step - 1), LANES - 1)
            below = jnp.take_along_axis(level, probe, axis=1) <= lane
            count = jnp.where(below & (count + step <= LANES), count + step, count)
            step //= 2
        upto = jnp.take_along_axis(mass[rows, :], jnp.maximum(count - 1, 0), axis=1)
        upto = jnp.where(count > 0, upto, 0.0)
        before = jnp.where(lane == 0, 0.0, pltpu.roll(upto, 1, 1))
        picked[rows, :] = upto - before
        return carry

    lax.fori_loop(0, home_cap // 8, sums, 0)

    def scatter(b, carry):
        at = pl.ds(column_ref[b], 1)
        cond_ref[at, :] = cond_ref[at, :] + picked[pl.ds(b, 1), :]
        return carry

    lax.fori_loop(0, live_count, scatter, 0)


def grow_blocks(column, position, live_count, table, level, planes):
    home_cap = level.shape[0]
    scratch = pltpu.VMEM((home_cap, LANES), jnp.float32)
    return pl.pallas_call(
        lambda *refs: grow_kernel(home_cap, *refs),
        out_shape=(
            jax.ShapeDtypeStruct(table.shape, jnp.float32),
            jax.ShapeDtypeStruct((home_cap, LANES), jnp.float32),
        ),
        in_specs=[SMEM, SMEM, SMEM, VMEM, VMEM, VMEM],
        out_specs=(VMEM, VMEM),
        scratch_shapes=[scratch, scratch, scratch],
        compiler_params=params(),
        cost_estimate=cost(8 << 20, 1 << 24),
        name="grow_blocks",
    )(column, position, live_count, table, level, planes)


def place_kernel(home_cap, send_cap, rows, source_ref, radius_ref, arrived_ref, out_ref):
    per_device = rows * send_cap

    def body(g, carry):
        for i in range(8):
            j = g * 8 + i
            source = source_ref[j]
            first = (source // send_cap) * per_device + source % send_cap
            block = arrived_ref[pl.ds(first, rows, stride=send_cap), :]
            out_ref[pl.ds(OWN_BLK + j, rows, stride=OWN_BLK), :] = block
            out_ref[pl.ds(j, 1), :] = radius_ref[pl.ds(source, 1), :]
        return carry

    lax.fori_loop(0, OWN_BLK // 8, body, 0)
    for r in range(3, 6):
        at = pl.ds(r * OWN_BLK, OWN_BLK)
        out_ref[at, :] = out_ref[at, :] + 0.1 * out_ref[pl.ds((r + 3) * OWN_BLK, OWN_BLK), :]


def place_blocks(source, radius, arrived, send_cap):
    home_cap = radius.shape[0]
    rows = arrived.shape[0] // home_cap
    return pl.pallas_call(
        lambda *refs: place_kernel(home_cap, send_cap, rows, *refs),
        out_shape=jax.ShapeDtypeStruct(((rows + 1) * OWN_BLK, LANES), jnp.float32),
        in_specs=[SMEM, VMEM, VMEM],
        out_specs=VMEM,
        compiler_params=params(),
        cost_estimate=cost(5 << 20, 1 << 20),
        name="place_blocks",
    )(source, radius, arrived)


def stencil_kernel(
    fields_ref,
    winds_ref,
    diff_ref,
    low_x,
    high_x,
    low_y,
    high_y,
    cond_ref,
    out_ref,
    ext,
    mid,
    coef,
):
    width = fields_ref.shape[1]
    merged = fields_ref.shape[2]
    lanes = merged + 2 * LANES
    core = slice(LANES, LANES + merged)
    inner = slice(ROW0, ROW0 + width)
    for k in range(9):
        if k < 5:
            own = fields_ref[k]
        elif k < 8:
            own = winds_ref[k - 5]
        else:
            own = diff_ref[...]
        ext[k, inner, core] = own
        ext[k, ROW0 - 2 : ROW0, core] = low_x[k]
        ext[k, ROW0 + width : ROW0 + width + 2, core] = high_x[k]
        ext[k, ROW0 - 2 : ROW0 + width + 2, 0:LANES] = low_y[k]
        ext[k, ROW0 - 2 : ROW0 + width + 2, LANES + merged : lanes] = high_y[k]

    chunks = range(ROW0 - 8, ROW0 + width + 8, 8)
    z = (lax.broadcasted_iota(jnp.int32, (8, lanes), 1) + (NZ - LANES % NZ)) % NZ
    top = z == NZ - 1
    bottom = z == 0

    def faces(c_low, c_high, k_low, k_high):
        courant = 0.5 * (c_low + c_high)
        diffuse = 0.5 * (k_low + k_high)
        return jnp.maximum(courant, 0.0) + diffuse, jnp.minimum(courant, 0.0) - diffuse

    def ahead(v, n):
        return pltpu.roll(v, lanes - n, 1)

    def behind(v, n):
        return pltpu.roll(v, n, 1)

    for base in chunks:
        rows = slice(base, base + 8)
        up = slice(base + 1, base + 9)
        down = slice(base - 1, base + 7)
        k0 = ext[8, rows, :]
        u0 = ext[5, rows, :]
        p, n = faces(u0, ext[5, up, :], k0, ext[8, up, :])
        p_low, n_low = faces(ext[5, down, :], u0, ext[8, down, :], k0)
        centre = 1.0 - (p - n_low)
        coef[0, rows, :] = -n
        coef[1, rows, :] = p_low
        v0 = ext[6, rows, :]
        p, n = faces(v0, ahead(v0, NZ), k0, ahead(k0, NZ))
        centre = centre - (p - behind(n, NZ))
        coef[2, rows, :] = -n
        coef[3, rows, :] = behind(p, NZ)
        w0 = ext[7, rows, :]
        p, n = faces(w0, ahead(w0, 1), k0, ahead(k0, 1))
        p = jnp.where(top, 0.0, p)
        n = jnp.where(top, 0.0, n)
        coef[4, rows, :] = -n
        p_low = jnp.where(bottom, 0.0, behind(p, 1))
        n_low = jnp.where(bottom, 0.0, behind(n, 1))
        coef[5, rows, :] = p_low
        coef[6, rows, :] = centre - (p - n_low)

    def update(src, f, base):
        rows = slice(base, base + 8)
        mine = src[f, rows, :]
        new = coef[6, rows, :] * mine
        new += coef[0, rows, :] * src[f, base + 1 : base + 9, :]
        new += coef[1, rows, :] * src[f, base - 1 : base + 7, :]
        new += coef[2, rows, :] * ahead(mine, NZ)
        new += coef[3, rows, :] * behind(mine, NZ)
        new += coef[4, rows, :] * ahead(mine, 1)
        new += coef[5, rows, :] * behind(mine, 1)
        return new

    def first(f, carry):
        for base in chunks:
            mid[f, base : base + 8, :] = update(ext, f, base)
        return carry

    lax.fori_loop(0, 5, first, 0)

    def second(f, carry):
        share = jnp.where(f == 0, 0.25, jnp.where(f == 1, -0.1, 0.0))
        for base in range(ROW0, ROW0 + width, 8):
            at = slice(base - ROW0, base - ROW0 + 8)
            out_ref[f, at, :] = update(mid, f, base)[:, core] + share * cond_ref[at, :]
        return carry

    lax.fori_loop(0, 5, second, 0)


def advance(fields, winds, diffusion, low_x, high_x, low_y, high_y, condensed):
    _, width, merged = fields.shape
    tall = ROW0 + width + 16
    wide = merged + 2 * LANES
    return pl.pallas_call(
        stencil_kernel,
        out_shape=jax.ShapeDtypeStruct(fields.shape, jnp.float32),
        in_specs=[VMEM] * 8,
        out_specs=VMEM,
        scratch_shapes=[
            pltpu.VMEM((9, tall, wide), jnp.float32),
            pltpu.VMEM((5, tall, wide), jnp.float32),
            pltpu.VMEM((7, tall, wide), jnp.float32),
        ],
        compiler_params=params(),
        cost_estimate=cost(16 << 20, 1 << 26),
        name="advance",
    )(fields, winds, diffusion, low_x, high_x, low_y, high_y, condensed)


def both_ways(low_edge, high_edge, axis):
    count = lax.axis_size(axis)
    return (
        lax.ppermute(high_edge, axis, [(i, (i + 1) % count) for i in range(count)]),
        lax.ppermute(low_edge, axis, [((i + 1) % count, i) for i in range(count)]),
    )


def per_device(fields, winds, diffusion, droplets, cells, balance_list):
    width = fields.shape[1]
    merged = fields.shape[2]
    home_cap = balance_list.shape[0]
    devices = lax.axis_size(("gx", "gy"))
    send_cap = home_cap // devices
    rows = droplets.shape[1] - 1
    column_count = width * merged // NZ

    def edge(xs, ys):
        grids = (fields, winds, diffusion[None])
        return jnp.concatenate([g[:, xs, ys] for g in grids], axis=0)

    every = slice(None)
    low_x, high_x = both_ways(
        edge(slice(0, 2), every), edge(slice(width - 2, width), every), "gx"
    )
    strip = 2 * NZ

    def side(ys):
        return jnp.concatenate([low_x[:, :, ys], edge(every, ys), high_x[:, :, ys]], axis=1)

    low_y, high_y = both_ways(side(slice(0, strip)), side(slice(merged - strip, merged)), "gy")
    low_y = jnp.pad(low_y, ((0, 0), (0, 0), (LANES - strip, 0)))
    high_y = jnp.pad(high_y, ((0, 0), (0, 0), (0, LANES - strip)))

    live = balance_list >= 0
    owner = jnp.where(live, balance_list // OWN_BLK, devices)
    slot = balance_list % OWN_BLK
    order = lax.iota(jnp.int32, home_cap)
    earlier = (owner[:, None] == owner[None, :]) & (order[None, :] < order[:, None])
    rank = jnp.sum(earlier.astype(jnp.int32), axis=1)
    position = jnp.where(live, owner * send_cap + rank, home_cap)
    base = jnp.where(live, owner * (send_cap * rows) + rank, 0)
    live_count = jnp.sum(live.astype(jnp.int32))[None]
    codes = (
        jnp.sum(
            jnp.where(position[None, :] == order[:, None], slot[None, :] + 1, 0), axis=1
        )
        - 1
    )
    planes = droplets.transpose(1, 0, 2).reshape((rows + 1) * home_cap, LANES)
    everyone = ("gx", "gy")

    def exchange(x):
        return lax.all_to_all(x, everyone, split_axis=0, concat_axis=0, tiled=True)

    arrived_codes = exchange(codes.reshape(devices, send_cap)).reshape(-1)
    outgoing = send_rows(base, live_count, planes, home_cap, send_cap)
    arrived = exchange(outgoing)

    level = cells % NZ
    column = cells[:, 0] // NZ
    gap = jnp.zeros((column_count, LANES // 2 - NZ), jnp.float32)
    table = jnp.concatenate(
        [
            fields[0].reshape(column_count, NZ),
            gap,
            fields[1].reshape(column_count, NZ),
            gap,
        ],
        axis=1,
    )
    condensed, radius = grow_blocks(column, position, live_count, table, level, planes)
    arrived_radius = exchange(radius)
    condensed = condensed[:, :NZ].reshape(width, merged)
    fields_out = advance(fields, winds, diffusion, low_x, high_x, low_y, high_y, condensed)

    own = lax.iota(jnp.int32, OWN_BLK)
    source = jnp.sum(
        jnp.where(arrived_codes[None, :] == own[:, None], order[None, :], 0), axis=1
    )
    placed = place_blocks(source, arrived_radius, arrived, send_cap)
    droplets_out = placed.reshape(rows + 1, OWN_BLK, LANES).transpose(1, 0, 2)
    return (fields_out, droplets_out)


def solution(mesh):
    return jax.shard_map(
        per_device,
        mesh=mesh,
        in_specs=(
            P(None, "gx", "gy"),
            P(None, "gx", "gy"),
            P("gx", "gy"),
            P(("gx", "gy"), None, None),
            P(("gx", "gy"), None),
            P(("gx", "gy")),
        ),
        out_specs=(P(None, "gx", "gy"), P(("gx", "gy"), None, None)),
        check_vma=False,
    )
```

```python
import jax
import jax.numpy as jnp
from jax import lax
from jax.experimental import pallas as pl
from jax.experimental.pallas import tpu as pltpu
from jax.sharding import PartitionSpec as P

NZ = 48
OWN_BLK = 256
SUBSTEPS = 4
LANES = 128
ROW0 = 16
BATCH = 64
VMEM = pl.BlockSpec(memory_space=pltpu.VMEM)
SMEM = pl.BlockSpec(memory_space=pltpu.SMEM)
LIMIT = 56 * 1024 * 1024


def params():
    return pltpu.CompilerParams(vmem_limit_bytes=LIMIT)


def cost(bytes_accessed, flops):
    return pl.CostEstimate(flops=flops, bytes_accessed=bytes_accessed, transcendentals=0)


CODE_ROWS = 8


def send_kernel(home_cap, send_cap, rows, source_ref, code_ref, drops_ref, out_ref):
    devices = home_cap // send_cap
    per_device = rows * send_cap + CODE_ROWS
    unroll = min(8, send_cap)

    def body(g, carry):
        start = (g // (send_cap // unroll)) * per_device + (g % (send_cap // unroll)) * unroll
        for i in range(unroll):
            b = source_ref[g * unroll + i]
            block = drops_ref[pl.ds(home_cap + b, rows, stride=home_cap), :]
            out_ref[pl.ds(start + i, rows, stride=send_cap), :] = block
        return carry

    lax.fori_loop(0, home_cap // unroll, body, 0)

    def codes(d, carry):
        out_ref[pl.ds(d * per_device + rows * send_cap, 1), :] = code_ref[pl.ds(d, 1), :]
        return carry

    lax.fori_loop(0, devices, codes, 0)


def send_rows(source, codes, planes, home_cap, send_cap):
    rows = planes.shape[0] // home_cap - 1
    devices = home_cap // send_cap
    total = devices * (rows * send_cap + CODE_ROWS)
    return pl.pallas_call(
        lambda *refs: send_kernel(home_cap, send_cap, rows, *refs),
        out_shape=jax.ShapeDtypeStruct((total, LANES), jnp.float32),
        in_specs=[SMEM, VMEM, VMEM],
        out_specs=VMEM,
        compiler_params=params(),
        cost_estimate=cost(6 << 20, 1 << 20),
        name="send_rows",
    )(source, codes, planes)


def grow_kernel(
    home_cap,
    column_ref,
    source_ref,
    live_ref,
    table_ref,
    level_ref,
    drops_ref,
    cond_ref,
    sent_ref,
    picked,
    radius_out,
    mass,
):
    live_count = live_ref[0]

    def fetch(g, carry):
        for i in range(8):
            b = g * 8 + i
            picked[pl.ds(b, 1), :] = table_ref[pl.ds(column_ref[b], 1), :]
        return carry

    lax.fori_loop(0, home_cap // 8, fetch, 0)

    def one(g, carry):
        at = pl.multiple_of(g * BATCH, BATCH)
        rows = pl.ds(at, BATCH)
        level = level_ref[rows, :]
        pair = picked[rows, :]
        theta = jnp.take_along_axis(pair, level, axis=1)
        vapour = jnp.take_along_axis(pair, level + 64, axis=1)
        supersat = vapour - 0.5 * jnp.tanh(theta)
        growth_rate = 1.0 / (1.0 + 0.1 * theta * theta)
        start = drops_ref[rows, :]
        solute = drops_ref[pl.ds(home_cap + at, BATCH), :]
        weight = drops_ref[pl.ds(2 * home_cap + at, BATCH), :]
        square = start * start
        for _ in range(SUBSTEPS):
            radius = jnp.sqrt(square)
            square = jnp.maximum(
                square
                + 0.05
                * growth_rate
                * (supersat - 0.02 / radius + solute / (radius * radius * radius)),
                0.04,
            )
        radius = jnp.sqrt(square)
        radius_out[rows, :] = radius
        grown = weight * (radius * square - start * start * start)
        block = at + lax.broadcasted_iota(jnp.int32, (BATCH, LANES), 0)
        mass[rows, :] = jnp.where(block < live_count, grown, 0.0)
        return carry

    lax.fori_loop(0, home_cap // BATCH, one, 0)

    def send(g, carry):
        for i in range(8):
            b = g * 8 + i
            sent_ref[pl.ds(b, 1), :] = radius_out[pl.ds(source_ref[b], 1), :]
        return carry

    lax.fori_loop(0, home_cap // 8, send, 0)
    row = lax.broadcasted_iota(jnp.int32, (LANES, LANES), 0)
    column = lax.broadcasted_iota(jnp.int32, (LANES, LANES), 1)
    upper = (row <= column).astype(jnp.float32)
    mass[...] = jnp.dot(
        mass[...], upper, precision=lax.Precision.HIGHEST, preferred_element_type=jnp.float32
    )
    cond_ref[...] = jnp.zeros_like(cond_ref)
    lane = lax.broadcasted_iota(jnp.int32, (BATCH, LANES), 1)

    def sums(g, carry):
        rows = pl.ds(pl.multiple_of(g * BATCH, BATCH), BATCH)
        level = level_ref[rows, :]
        count = jnp.zeros((BATCH, LANES), jnp.int32)
        step = LANES
        while step >= 1:
            probe = jnp.minimum(count + (step - 1), LANES - 1)
            below = jnp.take_along_axis(level, probe, axis=1) <= lane
            count = jnp.where(below & (count + step <= LANES), count + step, count)
            step //= 2
        upto = jnp.take_along_axis(mass[rows, :], jnp.maximum(count - 1, 0), axis=1)
        upto = jnp.where(count > 0, upto, 0.0)
        before = jnp.where(lane == 0, 0.0, pltpu.roll(upto, 1, 1))
        picked[rows, :] = upto - before
        return carry

    lax.fori_loop(0, home_cap // BATCH, sums, 0)

    def scatter(g, carry):
        for i in range(8):
            b = g * 8 + i
            at = pl.ds(column_ref[b], 1)
            cond_ref[at, :] = cond_ref[at, :] + picked[pl.ds(b, 1), :]
        return carry

    lax.fori_loop(0, home_cap // 8, scatter, 0)


def grow_blocks(column, source, live_count, table, level, planes):
    home_cap = level.shape[0]
    scratch = pltpu.VMEM((home_cap, LANES), jnp.float32)
    return pl.pallas_call(
        lambda *refs: grow_kernel(home_cap, *refs),
        out_shape=(
            jax.ShapeDtypeStruct(table.shape, jnp.float32),
            jax.ShapeDtypeStruct((home_cap, LANES), jnp.float32),
        ),
        in_specs=[SMEM, SMEM, SMEM, VMEM, VMEM, VMEM],
        out_specs=(VMEM, VMEM),
        scratch_shapes=[scratch, scratch, scratch],
        compiler_params=params(),
        cost_estimate=cost(8 << 20, 1 << 24),
        name="grow_blocks",
    )(column, source, live_count, table, level, planes)


def place_kernel(home_cap, send_cap, rows, source_ref, arrived_ref, out_ref):
    per_device = rows * send_cap + CODE_ROWS

    def body(g, carry):
        for i in range(8):
            j = g * 8 + i
            source = source_ref[j]
            first = (source // send_cap) * per_device + source % send_cap
            block = arrived_ref[pl.ds(first, rows, stride=send_cap), :]
            out_ref[pl.ds(OWN_BLK + j, rows, stride=OWN_BLK), :] = block
        return carry

    lax.fori_loop(0, OWN_BLK // 8, body, 0)
    for r in range(3, 6):
        at = pl.ds(r * OWN_BLK, OWN_BLK)
        out_ref[at, :] = out_ref[at, :] + 0.1 * out_ref[pl.ds((r + 3) * OWN_BLK, OWN_BLK), :]


def place_blocks(source, arrived, home_cap, send_cap, rows):
    return pl.pallas_call(
        lambda *refs: place_kernel(home_cap, send_cap, rows, *refs),
        out_shape=jax.ShapeDtypeStruct(((rows + 1) * OWN_BLK, LANES), jnp.float32),
        in_specs=[SMEM, VMEM],
        out_specs=VMEM,
        compiler_params=params(),
        cost_estimate=cost(5 << 20, 1 << 20),
        name="place_blocks",
    )(source, arrived)


def place_radius_kernel(source_ref, radius_ref, placed_ref, out_ref, rows_ref, sem):
    def body(g, carry):
        for i in range(8):
            j = g * 8 + i
            rows_ref[pl.ds(j, 1), :] = radius_ref[pl.ds(source_ref[j], 1), :]
        return carry

    lax.fori_loop(0, OWN_BLK // 8, body, 0)
    copy = pltpu.make_async_copy(rows_ref, out_ref.at[pl.ds(0, OWN_BLK), :], sem)
    copy.start()
    copy.wait()


def place_radius(source, radius, placed):
    return pl.pallas_call(
        place_radius_kernel,
        out_shape=jax.ShapeDtypeStruct(placed.shape, jnp.float32),
        in_specs=[SMEM, VMEM, pl.BlockSpec(memory_space=pl.ANY)],
        out_specs=pl.BlockSpec(memory_space=pl.ANY),
        scratch_shapes=[pltpu.VMEM((OWN_BLK, LANES), jnp.float32), pltpu.SemaphoreType.DMA],
        input_output_aliases={2: 0},
        compiler_params=params(),
        cost_estimate=cost(1 << 19, 1 << 16),
        name="place_radius",
    )(source, radius, placed)


def stencil_kernel(
    fields_ref,
    winds_ref,
    diff_ref,
    low_x,
    high_x,
    low_y,
    high_y,
    cond_ref,
    out_ref,
    ext,
    mid,
    coef,
):
    width = fields_ref.shape[1]
    merged = fields_ref.shape[2]
    lanes = merged + 2 * LANES
    core = slice(LANES, LANES + merged)
    inner = slice(ROW0, ROW0 + width)
    for k in range(9):
        if k < 5:
            own = fields_ref[k]
        elif k < 8:
            own = winds_ref[k - 5]
        else:
            own = diff_ref[...]
        ext[k, inner, core] = own
        ext[k, ROW0 - 2 : ROW0, core] = low_x[k]
        ext[k, ROW0 + width : ROW0 + width + 2, core] = high_x[k]
        ext[k, ROW0 - 2 : ROW0 + width + 2, 0:LANES] = low_y[k]
        ext[k, ROW0 - 2 : ROW0 + width + 2, LANES + merged : lanes] = high_y[k]

    chunks = range(ROW0 - 8, ROW0 + width + 8, 8)
    z = (lax.broadcasted_iota(jnp.int32, (8, lanes), 1) + (NZ - LANES % NZ)) % NZ
    top = z == NZ - 1
    bottom = z == 0

    def faces(c_low, c_high, k_low, k_high):
        courant = 0.5 * (c_low + c_high)
        diffuse = 0.5 * (k_low + k_high)
        return jnp.maximum(courant, 0.0) + diffuse, jnp.minimum(courant, 0.0) - diffuse

    def ahead(v, n):
        return pltpu.roll(v, lanes - n, 1)

    def behind(v, n):
        return pltpu.roll(v, n, 1)

    for base in chunks:
        rows = slice(base, base + 8)
        up = slice(base + 1, base + 9)
        down = slice(base - 1, base + 7)
        k0 = ext[8, rows, :]
        u0 = ext[5, rows, :]
        p, n = faces(u0, ext[5, up, :], k0, ext[8, up, :])
        p_low, n_low = faces(ext[5, down, :], u0, ext[8, down, :], k0)
        centre = 1.0 - (p - n_low)
        coef[0, rows, :] = -n
        coef[1, rows, :] = p_low
        v0 = ext[6, rows, :]
        p, n = faces(v0, ahead(v0, NZ), k0, ahead(k0, NZ))
        centre = centre - (p - behind(n, NZ))
        coef[2, rows, :] = -n
        coef[3, rows, :] = behind(p, NZ)
        w0 = ext[7, rows, :]
        p, n = faces(w0, ahead(w0, 1), k0, ahead(k0, 1))
        p = jnp.where(top, 0.0, p)
        n = jnp.where(top, 0.0, n)
        coef[4, rows, :] = -n
        p_low = jnp.where(bottom, 0.0, behind(p, 1))
        n_low = jnp.where(bottom, 0.0, behind(n, 1))
        coef[5, rows, :] = p_low
        coef[6, rows, :] = centre - (p - n_low)

    def update(src, f, base):
        rows = slice(base, base + 8)
        mine = src[f, rows, :]
        new = coef[6, rows, :] * mine
        new += coef[0, rows, :] * src[f, base + 1 : base + 9, :]
        new += coef[1, rows, :] * src[f, base - 1 : base + 7, :]
        new += coef[2, rows, :] * ahead(mine, NZ)
        new += coef[3, rows, :] * behind(mine, NZ)
        new += coef[4, rows, :] * ahead(mine, 1)
        new += coef[5, rows, :] * behind(mine, 1)
        return new

    def first(f, carry):
        for base in chunks:
            mid[f, base : base + 8, :] = update(ext, f, base)
        return carry

    lax.fori_loop(0, 5, first, 0)

    def second(f, carry):
        share = jnp.where(f == 0, 0.25, jnp.where(f == 1, -0.1, 0.0))
        for base in range(ROW0, ROW0 + width, 8):
            at = slice(base - ROW0, base - ROW0 + 8)
            out_ref[f, at, :] = update(mid, f, base)[:, core] + share * cond_ref[at, :]
        return carry

    lax.fori_loop(0, 5, second, 0)


def advance(fields, winds, diffusion, low_x, high_x, low_y, high_y, condensed):
    _, width, merged = fields.shape
    tall = ROW0 + width + 16
    wide = merged + 2 * LANES
    return pl.pallas_call(
        stencil_kernel,
        out_shape=jax.ShapeDtypeStruct(fields.shape, jnp.float32),
        in_specs=[VMEM] * 8,
        out_specs=VMEM,
        scratch_shapes=[
            pltpu.VMEM((9, tall, wide), jnp.float32),
            pltpu.VMEM((5, tall, wide), jnp.float32),
            pltpu.VMEM((7, tall, wide), jnp.float32),
        ],
        compiler_params=params(),
        cost_estimate=cost(16 << 20, 1 << 26),
        name="advance",
    )(fields, winds, diffusion, low_x, high_x, low_y, high_y, condensed)


def both_ways(low_edge, high_edge, axis):
    count = lax.axis_size(axis)
    return (
        lax.ppermute(high_edge, axis, [(i, (i + 1) % count) for i in range(count)]),
        lax.ppermute(low_edge, axis, [((i + 1) % count, i) for i in range(count)]),
    )


def per_device(fields, winds, diffusion, droplets, cells, balance_list):
    width = fields.shape[1]
    merged = fields.shape[2]
    home_cap = balance_list.shape[0]
    devices = lax.axis_size(("gx", "gy"))
    send_cap = home_cap // devices
    rows = droplets.shape[1] - 1
    column_count = width * merged // NZ

    def edge(xs, ys):
        grids = (fields, winds, diffusion[None])
        return jnp.concatenate([g[:, xs, ys] for g in grids], axis=0)

    every = slice(None)
    x_edges = (edge(slice(0, 2), every), edge(slice(width - 2, width), every))
    x_edges, balance_list = lax.optimization_barrier((x_edges, balance_list))
    low_x, high_x = both_ways(*x_edges, "gx")
    strip = 2 * NZ

    live = balance_list >= 0
    owner = jnp.where(live, balance_list // OWN_BLK, devices)
    slot = balance_list % OWN_BLK
    order = lax.iota(jnp.int32, home_cap)
    earlier = (owner[:, None] == owner[None, :]) & (order[None, :] < order[:, None])
    rank = jnp.sum(earlier.astype(jnp.int32), axis=1)
    position = jnp.where(live, owner * send_cap + rank, home_cap)
    live_count = jnp.sum(live.astype(jnp.int32))[None]
    taken = position[None, :] == order[:, None]
    send_source = jnp.sum(jnp.where(taken, order[None, :], 0), axis=1)
    codes = jnp.sum(jnp.where(taken, slot[None, :] + 1, 0), axis=1) - 1
    codes = codes.astype(jnp.float32).reshape(devices, send_cap)
    codes = jnp.pad(codes, ((0, 0), (0, LANES - send_cap)))
    planes = droplets.transpose(1, 0, 2).reshape((rows + 1) * home_cap, LANES)
    everyone = ("gx", "gy")

    def side(ys):
        return jnp.concatenate([low_x[:, :, ys], edge(every, ys), high_x[:, :, ys]], axis=1)

    sides = (side(slice(0, strip)), side(slice(merged - strip, merged)))
    sides, send_source = lax.optimization_barrier((sides, send_source))
    low_y, high_y = both_ways(*sides, "gy")

    def exchange(x):
        return lax.all_to_all(x, everyone, split_axis=0, concat_axis=0, tiled=True)

    outgoing = send_rows(send_source, codes, planes, home_cap, send_cap)
    outgoing, low_y, high_y, column = lax.optimization_barrier(
        (outgoing, low_y, high_y, cells[:, 0] // NZ)
    )
    arrived = exchange(outgoing)
    low_y = jnp.pad(low_y, ((0, 0), (0, 0), (LANES - strip, 0)))
    high_y = jnp.pad(high_y, ((0, 0), (0, 0), (0, LANES - strip)))

    level = cells % NZ
    gap = jnp.zeros((column_count, LANES // 2 - NZ), jnp.float32)
    table = jnp.concatenate(
        [
            fields[0].reshape(column_count, NZ),
            gap,
            fields[1].reshape(column_count, NZ),
            gap,
        ],
        axis=1,
    )
    condensed, radius = grow_blocks(column, send_source, live_count, table, level, planes)
    condensed = condensed[:, :NZ].reshape(width, merged)
    fields_out = advance(fields, winds, diffusion, low_x, high_x, low_y, high_y, condensed)

    arrived, radius, fields_out = lax.optimization_barrier((arrived, radius, fields_out))
    arrived_radius = exchange(radius)
    per_device_rows = arrived.shape[0] // devices
    arrived_codes = arrived.reshape(devices, per_device_rows, LANES)[
        :, rows * send_cap, :send_cap
    ].reshape(-1)
    own = lax.iota(jnp.int32, OWN_BLK).astype(jnp.float32)
    source = jnp.sum(
        jnp.where(arrived_codes[None, :] == own[:, None], order[None, :], 0), axis=1
    )
    placed = place_blocks(source, arrived, home_cap, send_cap, rows)
    placed = place_radius(source, arrived_radius, placed)
    droplets_out = placed.reshape(rows + 1, OWN_BLK, LANES).transpose(1, 0, 2)
    return (fields_out, droplets_out)


def solution(mesh):
    return jax.shard_map(
        per_device,
        mesh=mesh,
        in_specs=(
            P(None, "gx", "gy"),
            P(None, "gx", "gy"),
            P("gx", "gy"),
            P(("gx", "gy"), None, None),
            P(("gx", "gy"), None),
            P(("gx", "gy")),
        ),
        out_specs=(P(None, "gx", "gy"), P(("gx", "gy"), None, None)),
        check_vma=False,
    )
```

```python
import jax
import jax.numpy as jnp
from jax import lax
from jax.experimental import pallas as pl
from jax.experimental.pallas import tpu as pltpu
from jax.sharding import PartitionSpec as P

NZ = 48
OWN_BLK = 256
SUBSTEPS = 4
LANES = 128
ROW0 = 16
BATCH = 64
VMEM = pl.BlockSpec(memory_space=pltpu.VMEM)
SMEM = pl.BlockSpec(memory_space=pltpu.SMEM)
LIMIT = 56 * 1024 * 1024


def params():
    return pltpu.CompilerParams(vmem_limit_bytes=LIMIT)


def cost(bytes_accessed, flops):
    return pl.CostEstimate(flops=flops, bytes_accessed=bytes_accessed, transcendentals=0)


CODE_ROWS = 8


def send_kernel(home_cap, send_cap, rows, steps, source_ref, code_ref, drops_ref, out_ref):
    devices = home_cap // send_cap // steps
    per_device = rows * send_cap + CODE_ROWS
    first = pl.program_id(0) * devices

    def body(d, carry):
        start = d * per_device
        for i in range(send_cap):
            b = source_ref[(first + d) * send_cap + i]
            block = drops_ref[pl.ds(home_cap + b, rows, stride=home_cap), :]
            out_ref[pl.ds(start + i, rows, stride=send_cap), :] = block
        out_ref[pl.ds(start + rows * send_cap, 1), :] = code_ref[pl.ds(first + d, 1), :]
        return carry

    lax.fori_loop(0, devices, body, 0)


def send_rows(source, codes, planes, home_cap, send_cap):
    rows = planes.shape[0] // home_cap - 1
    devices = home_cap // send_cap
    total = devices * (rows * send_cap + CODE_ROWS)
    steps = 4
    return pl.pallas_call(
        lambda *refs: send_kernel(home_cap, send_cap, rows, steps, *refs),
        grid=(steps,),
        out_shape=jax.ShapeDtypeStruct((total, LANES), jnp.float32),
        in_specs=[SMEM, VMEM, VMEM],
        out_specs=pl.BlockSpec((total // steps, LANES), lambda i: (i, 0)),
        compiler_params=params(),
        cost_estimate=cost(6 << 20, 1 << 20),
        name="send_rows",
    )(source, codes, planes)


def grow_kernel(
    home_cap,
    column_ref,
    source_ref,
    live_ref,
    table_ref,
    level_ref,
    drops_ref,
    cond_ref,
    sent_ref,
    picked,
    radius_out,
    mass,
):
    live_count = live_ref[0]

    def fetch(g, carry):
        for i in range(8):
            b = g * 8 + i
            picked[pl.ds(b, 1), :] = table_ref[pl.ds(column_ref[b], 1), :]
        return carry

    lax.fori_loop(0, home_cap // 8, fetch, 0)

    def one(g, carry):
        at = pl.multiple_of(g * BATCH, BATCH)
        rows = pl.ds(at, BATCH)
        level = level_ref[rows, :]
        pair = picked[rows, :]
        theta = jnp.take_along_axis(pair, level, axis=1)
        vapour = jnp.take_along_axis(pair, level + 64, axis=1)
        supersat = vapour - 0.5 * jnp.tanh(theta)
        growth_rate = 1.0 / (1.0 + 0.1 * theta * theta)
        start = drops_ref[rows, :]
        solute = drops_ref[pl.ds(home_cap + at, BATCH), :]
        weight = drops_ref[pl.ds(2 * home_cap + at, BATCH), :]
        square = start * start
        for _ in range(SUBSTEPS):
            radius = jnp.sqrt(square)
            square = jnp.maximum(
                square
                + 0.05
                * growth_rate
                * (supersat - 0.02 / radius + solute / (radius * radius * radius)),
                0.04,
            )
        radius = jnp.sqrt(square)
        radius_out[rows, :] = radius
        grown = weight * (radius * square - start * start * start)
        block = at + lax.broadcasted_iota(jnp.int32, (BATCH, LANES), 0)
        mass[rows, :] = jnp.where(block < live_count, grown, 0.0)
        return carry

    lax.fori_loop(0, home_cap // BATCH, one, 0)

    def send(g, carry):
        for i in range(8):
            b = g * 8 + i
            sent_ref[pl.ds(b, 1), :] = radius_out[pl.ds(source_ref[b], 1), :]
        return carry

    lax.fori_loop(0, home_cap // 8, send, 0)
    row = lax.broadcasted_iota(jnp.int32, (LANES, LANES), 0)
    column = lax.broadcasted_iota(jnp.int32, (LANES, LANES), 1)
    upper = (row <= column).astype(jnp.float32)
    mass[...] = jnp.dot(
        mass[...], upper, precision=lax.Precision.HIGHEST, preferred_element_type=jnp.float32
    )
    cond_ref[...] = jnp.zeros_like(cond_ref)
    lane = lax.broadcasted_iota(jnp.int32, (BATCH, LANES), 1)

    def sums(g, carry):
        rows = pl.ds(pl.multiple_of(g * BATCH, BATCH), BATCH)
        level = level_ref[rows, :]
        count = jnp.zeros((BATCH, LANES), jnp.int32)
        step = LANES
        while step >= 1:
            probe = jnp.minimum(count + (step - 1), LANES - 1)
            below = jnp.take_along_axis(level, probe, axis=1) <= lane
            count = jnp.where(below & (count + step <= LANES), count + step, count)
            step //= 2
        upto = jnp.take_along_axis(mass[rows, :], jnp.maximum(count - 1, 0), axis=1)
        upto = jnp.where(count > 0, upto, 0.0)
        before = jnp.where(lane == 0, 0.0, pltpu.roll(upto, 1, 1))
        picked[rows, :] = upto - before
        return carry

    lax.fori_loop(0, home_cap // BATCH, sums, 0)

    def scatter(g, carry):
        for i in range(8):
            b = g * 8 + i
            at = pl.ds(column_ref[b], 1)
            cond_ref[at, :] = cond_ref[at, :] + picked[pl.ds(b, 1), :]
        return carry

    lax.fori_loop(0, home_cap // 8, scatter, 0)


def grow_blocks(column, source, live_count, table, level, planes):
    home_cap = level.shape[0]
    scratch = pltpu.VMEM((home_cap, LANES), jnp.float32)
    return pl.pallas_call(
        lambda *refs: grow_kernel(home_cap, *refs),
        out_shape=(
            jax.ShapeDtypeStruct(table.shape, jnp.float32),
            jax.ShapeDtypeStruct((home_cap, LANES), jnp.float32),
        ),
        in_specs=[SMEM, SMEM, SMEM, VMEM, VMEM, VMEM],
        out_specs=(VMEM, VMEM),
        scratch_shapes=[scratch, scratch, scratch],
        compiler_params=params(),
        cost_estimate=cost(8 << 20, 1 << 24),
        name="grow_blocks",
    )(column, source, live_count, table, level, planes)


def place_kernel(home_cap, send_cap, rows, source_ref, arrived_ref, out_ref):
    per_device = rows * send_cap + CODE_ROWS

    def body(g, carry):
        for i in range(8):
            j = g * 8 + i
            source = source_ref[j]
            first = (source // send_cap) * per_device + source % send_cap
            block = arrived_ref[pl.ds(first, rows, stride=send_cap), :]
            out_ref[pl.ds(OWN_BLK + j, rows, stride=OWN_BLK), :] = block
        return carry

    lax.fori_loop(0, OWN_BLK // 8, body, 0)
    for r in range(3, 6):
        at = pl.ds(r * OWN_BLK, OWN_BLK)
        out_ref[at, :] = out_ref[at, :] + 0.1 * out_ref[pl.ds((r + 3) * OWN_BLK, OWN_BLK), :]


def place_blocks(source, arrived, home_cap, send_cap, rows):
    return pl.pallas_call(
        lambda *refs: place_kernel(home_cap, send_cap, rows, *refs),
        out_shape=jax.ShapeDtypeStruct(((rows + 1) * OWN_BLK, LANES), jnp.float32),
        in_specs=[SMEM, VMEM],
        out_specs=VMEM,
        compiler_params=params(),
        cost_estimate=cost(5 << 20, 1 << 20),
        name="place_blocks",
    )(source, arrived)


def place_radius_kernel(source_ref, radius_ref, placed_ref, out_ref, rows_ref, sem):
    def body(g, carry):
        for i in range(8):
            j = g * 8 + i
            rows_ref[pl.ds(j, 1), :] = radius_ref[pl.ds(source_ref[j], 1), :]
        return carry

    lax.fori_loop(0, OWN_BLK // 8, body, 0)
    copy = pltpu.make_async_copy(rows_ref, out_ref.at[pl.ds(0, OWN_BLK), :], sem)
    copy.start()
    copy.wait()


def place_radius(source, radius, placed):
    return pl.pallas_call(
        place_radius_kernel,
        out_shape=jax.ShapeDtypeStruct(placed.shape, jnp.float32),
        in_specs=[SMEM, VMEM, pl.BlockSpec(memory_space=pl.ANY)],
        out_specs=pl.BlockSpec(memory_space=pl.ANY),
        scratch_shapes=[pltpu.VMEM((OWN_BLK, LANES), jnp.float32), pltpu.SemaphoreType.DMA],
        input_output_aliases={2: 0},
        compiler_params=params(),
        cost_estimate=cost(1 << 19, 1 << 16),
        name="place_radius",
    )(source, radius, placed)


def stencil_kernel(
    fields_ref,
    winds_ref,
    diff_ref,
    low_x,
    high_x,
    low_y,
    high_y,
    cond_ref,
    out_ref,
    ext,
    mid,
    coef,
):
    width = fields_ref.shape[1]
    merged = fields_ref.shape[2]
    lanes = merged + 2 * LANES
    core = slice(LANES, LANES + merged)
    inner = slice(ROW0, ROW0 + width)
    for k in range(9):
        if k < 5:
            own = fields_ref[k]
        elif k < 8:
            own = winds_ref[k - 5]
        else:
            own = diff_ref[...]
        ext[k, inner, core] = own
        ext[k, ROW0 - 2 : ROW0, core] = low_x[k]
        ext[k, ROW0 + width : ROW0 + width + 2, core] = high_x[k]
        ext[k, ROW0 - 2 : ROW0 + width + 2, 0:LANES] = low_y[k]
        ext[k, ROW0 - 2 : ROW0 + width + 2, LANES + merged : lanes] = high_y[k]

    chunks = range(ROW0 - 8, ROW0 + width + 8, 8)
    z = (lax.broadcasted_iota(jnp.int32, (8, lanes), 1) + (NZ - LANES % NZ)) % NZ
    top = z == NZ - 1
    bottom = z == 0

    def faces(c_low, c_high, k_low, k_high):
        courant = 0.5 * (c_low + c_high)
        diffuse = 0.5 * (k_low + k_high)
        return jnp.maximum(courant, 0.0) + diffuse, jnp.minimum(courant, 0.0) - diffuse

    def ahead(v, n):
        return pltpu.roll(v, lanes - n, 1)

    def behind(v, n):
        return pltpu.roll(v, n, 1)

    for base in chunks:
        rows = slice(base, base + 8)
        up = slice(base + 1, base + 9)
        down = slice(base - 1, base + 7)
        k0 = ext[8, rows, :]
        u0 = ext[5, rows, :]
        p, n = faces(u0, ext[5, up, :], k0, ext[8, up, :])
        p_low, n_low = faces(ext[5, down, :], u0, ext[8, down, :], k0)
        centre = 1.0 - (p - n_low)
        coef[0, rows, :] = -n
        coef[1, rows, :] = p_low
        v0 = ext[6, rows, :]
        p, n = faces(v0, ahead(v0, NZ), k0, ahead(k0, NZ))
        centre = centre - (p - behind(n, NZ))
        coef[2, rows, :] = -n
        coef[3, rows, :] = behind(p, NZ)
        w0 = ext[7, rows, :]
        p, n = faces(w0, ahead(w0, 1), k0, ahead(k0, 1))
        p = jnp.where(top, 0.0, p)
        n = jnp.where(top, 0.0, n)
        coef[4, rows, :] = -n
        p_low = jnp.where(bottom, 0.0, behind(p, 1))
        n_low = jnp.where(bottom, 0.0, behind(n, 1))
        coef[5, rows, :] = p_low
        coef[6, rows, :] = centre - (p - n_low)

    def update(src, f, base):
        rows = slice(base, base + 8)
        mine = src[f, rows, :]
        new = coef[6, rows, :] * mine
        new += coef[0, rows, :] * src[f, base + 1 : base + 9, :]
        new += coef[1, rows, :] * src[f, base - 1 : base + 7, :]
        new += coef[2, rows, :] * ahead(mine, NZ)
        new += coef[3, rows, :] * behind(mine, NZ)
        new += coef[4, rows, :] * ahead(mine, 1)
        new += coef[5, rows, :] * behind(mine, 1)
        return new

    def first(f, carry):
        for base in chunks:
            mid[f, base : base + 8, :] = update(ext, f, base)
        return carry

    lax.fori_loop(0, 5, first, 0)

    def second(f, carry):
        share = jnp.where(f == 0, 0.25, jnp.where(f == 1, -0.1, 0.0))
        for base in range(ROW0, ROW0 + width, 8):
            at = slice(base - ROW0, base - ROW0 + 8)
            out_ref[f, at, :] = update(mid, f, base)[:, core] + share * cond_ref[at, :]
        return carry

    lax.fori_loop(0, 5, second, 0)


def advance(fields, winds, diffusion, low_x, high_x, low_y, high_y, condensed):
    _, width, merged = fields.shape
    tall = ROW0 + width + 16
    wide = merged + 2 * LANES
    return pl.pallas_call(
        stencil_kernel,
        out_shape=jax.ShapeDtypeStruct(fields.shape, jnp.float32),
        in_specs=[VMEM] * 8,
        out_specs=VMEM,
        scratch_shapes=[
            pltpu.VMEM((9, tall, wide), jnp.float32),
            pltpu.VMEM((5, tall, wide), jnp.float32),
            pltpu.VMEM((7, tall, wide), jnp.float32),
        ],
        compiler_params=params(),
        cost_estimate=cost(16 << 20, 1 << 26),
        name="advance",
    )(fields, winds, diffusion, low_x, high_x, low_y, high_y, condensed)


def both_ways(low_edge, high_edge, axis):
    count = lax.axis_size(axis)
    return (
        lax.ppermute(high_edge, axis, [(i, (i + 1) % count) for i in range(count)]),
        lax.ppermute(low_edge, axis, [((i + 1) % count, i) for i in range(count)]),
    )


def per_device(fields, winds, diffusion, droplets, cells, balance_list):
    width = fields.shape[1]
    merged = fields.shape[2]
    home_cap = balance_list.shape[0]
    devices = lax.axis_size(("gx", "gy"))
    send_cap = home_cap // devices
    rows = droplets.shape[1] - 1
    column_count = width * merged // NZ

    every = slice(None)
    strip = 2 * NZ
    live = balance_list >= 0
    owner = jnp.where(live, balance_list // OWN_BLK, devices)
    slot = balance_list % OWN_BLK
    order = lax.iota(jnp.int32, home_cap)
    earlier = (owner[:, None] == owner[None, :]) & (order[None, :] < order[:, None])
    rank = jnp.sum(earlier.astype(jnp.int32), axis=1)
    position = jnp.where(live, owner * send_cap + rank, home_cap)
    live_count = jnp.sum(live.astype(jnp.int32))[None]
    taken = position[None, :] == order[:, None]
    send_source = jnp.sum(jnp.where(taken, order[None, :], 0), axis=1)
    codes = jnp.sum(jnp.where(taken, slot[None, :] + 1, 0), axis=1) - 1
    codes = codes.astype(jnp.float32).reshape(devices, send_cap)
    codes = jnp.pad(codes, ((0, 0), (0, LANES - send_cap)))
    planes = droplets.transpose(1, 0, 2).reshape((rows + 1) * home_cap, LANES)
    everyone = ("gx", "gy")

    def exchange(x):
        return lax.all_to_all(x, everyone, split_axis=0, concat_axis=0, tiled=True)

    outgoing = send_rows(send_source, codes, planes, home_cap, send_cap)
    outgoing, fields, winds, diffusion, cells = lax.optimization_barrier(
        (outgoing, fields, winds, diffusion, cells)
    )
    arrived = exchange(outgoing)

    def edge(xs, ys):
        grids = (fields, winds, diffusion[None])
        return jnp.concatenate([g[:, xs, ys] for g in grids], axis=0)

    low_x, high_x = both_ways(
        edge(slice(0, 2), every), edge(slice(width - 2, width), every), "gx"
    )

    def side(ys):
        return jnp.concatenate([low_x[:, :, ys], edge(every, ys), high_x[:, :, ys]], axis=1)

    sides = (side(slice(0, strip)), side(slice(merged - strip, merged)))
    sides, column = lax.optimization_barrier((sides, cells[:, 0] // NZ))
    low_y, high_y = both_ways(*sides, "gy")
    low_y = jnp.pad(low_y, ((0, 0), (0, 0), (LANES - strip, 0)))
    high_y = jnp.pad(high_y, ((0, 0), (0, 0), (0, LANES - strip)))

    level = cells % NZ
    gap = jnp.zeros((column_count, LANES // 2 - NZ), jnp.float32)
    table = jnp.concatenate(
        [
            fields[0].reshape(column_count, NZ),
            gap,
            fields[1].reshape(column_count, NZ),
            gap,
        ],
        axis=1,
    )
    condensed, radius = grow_blocks(column, send_source, live_count, table, level, planes)
    condensed = condensed[:, :NZ].reshape(width, merged)
    fields_out = advance(fields, winds, diffusion, low_x, high_x, low_y, high_y, condensed)

    arrived, radius, fields_out = lax.optimization_barrier((arrived, radius, fields_out))
    arrived_radius = exchange(radius)
    per_device_rows = arrived.shape[0] // devices
    arrived_codes = arrived.reshape(devices, per_device_rows, LANES)[
        :, rows * send_cap, :send_cap
    ].reshape(-1)
    own = lax.iota(jnp.int32, OWN_BLK).astype(jnp.float32)
    source = jnp.sum(
        jnp.where(arrived_codes[None, :] == own[:, None], order[None, :], 0), axis=1
    )
    placed = place_blocks(source, arrived, home_cap, send_cap, rows)
    placed = place_radius(source, arrived_radius, placed)
    droplets_out = placed.reshape(rows + 1, OWN_BLK, LANES).transpose(1, 0, 2)
    return (fields_out, droplets_out)


def solution(mesh):
    return jax.shard_map(
        per_device,
        mesh=mesh,
        in_specs=(
            P(None, "gx", "gy"),
            P(None, "gx", "gy"),
            P("gx", "gy"),
            P(("gx", "gy"), None, None),
            P(("gx", "gy"), None),
            P(("gx", "gy")),
        ),
        out_specs=(P(None, "gx", "gy"), P(("gx", "gy"), None, None)),
        check_vma=False,
    )
```

```python
import jax
import jax.numpy as jnp
from jax import lax
from jax.experimental import pallas as pl
from jax.experimental.pallas import tpu as pltpu
from jax.sharding import PartitionSpec as P

NZ = 48
OWN_BLK = 256
SUBSTEPS = 4
LANES = 128
ROW0 = 16
BATCH = 64
VMEM = pl.BlockSpec(memory_space=pltpu.VMEM)
SMEM = pl.BlockSpec(memory_space=pltpu.SMEM)
LIMIT = 56 * 1024 * 1024


def params():
    return pltpu.CompilerParams(vmem_limit_bytes=LIMIT)


def cost(bytes_accessed, flops):
    return pl.CostEstimate(flops=flops, bytes_accessed=bytes_accessed, transcendentals=0)


CODE_ROWS = 8
HALF = 6


def pack_kernel(f_low, f_high, w_low, w_high, d_low, d_high, low_ref, high_ref):
    for f, w, d, out in ((f_low, w_low, d_low, low_ref), (f_high, w_high, d_high, high_ref)):
        out[0:5] = f[...]
        out[5:8] = w[...]
        out[8] = d[...]


def pack_sides(fields, winds, diffusion):
    _, width, merged = fields.shape
    last = merged // LANES - 1
    specs = []
    for count in (5, 3):
        for at in (0, last):
            specs.append(pl.BlockSpec((count, width, LANES), lambda i, at=at: (0, 0, at)))
    for at in (0, last):
        specs.append(pl.BlockSpec((width, LANES), lambda i, at=at: (0, at)))
    shape = jax.ShapeDtypeStruct((9, width, LANES), jnp.float32)
    whole = pl.BlockSpec((9, width, LANES), lambda i: (0, 0, 0))
    return pl.pallas_call(
        pack_kernel,
        grid=(1,),
        out_shape=(shape, shape),
        in_specs=specs,
        out_specs=(whole, whole),
        cost_estimate=cost(1 << 20, 1 << 10),
        name="pack_sides",
    )(fields, fields, winds, winds, diffusion, diffusion)


def send_kernel(home_cap, send_cap, steps, source_ref, code_ref, drops_ref, out_ref):
    devices = home_cap // send_cap // steps
    per_device = HALF * send_cap + CODE_ROWS
    first = pl.program_id(0) * devices

    def body(d, carry):
        start = d * per_device
        for i in range(send_cap):
            b = source_ref[(first + d) * send_cap + i]
            block = drops_ref[pl.ds(b, HALF, stride=home_cap), :]
            out_ref[pl.ds(start + i, HALF, stride=send_cap), :] = block
        out_ref[pl.ds(start + HALF * send_cap, 1), :] = code_ref[pl.ds(first + d, 1), :]
        return carry

    lax.fori_loop(0, devices, body, 0)


def send_rows(source, codes, planes, home_cap, send_cap):
    devices = home_cap // send_cap
    total = devices * (HALF * send_cap + CODE_ROWS)
    steps = 4
    return pl.pallas_call(
        lambda *refs: send_kernel(home_cap, send_cap, steps, *refs),
        grid=(steps,),
        out_shape=jax.ShapeDtypeStruct((total, LANES), jnp.float32),
        in_specs=[SMEM, VMEM, pl.BlockSpec((HALF * home_cap, LANES), lambda i: (1, 0))],
        out_specs=pl.BlockSpec((total // steps, LANES), lambda i: (i, 0)),
        compiler_params=params(),
        cost_estimate=cost(3 << 20, 1 << 20),
        name="send_rows",
    )(source, codes, planes)


def grow_kernel(
    home_cap,
    send_cap,
    column_ref,
    source_ref,
    live_ref,
    table_ref,
    level_ref,
    drops_ref,
    cond_ref,
    sent_ref,
    picked,
    moved,
    mass,
):
    live_count = live_ref[0]

    def fetch(g, carry):
        for i in range(8):
            b = g * 8 + i
            picked[pl.ds(b, 1), :] = table_ref[pl.ds(column_ref[b], 1), :]
        return carry

    lax.fori_loop(0, home_cap // 8, fetch, 0)

    def one(g, carry):
        at = pl.multiple_of(g * BATCH, BATCH)
        rows = pl.ds(at, BATCH)
        level = level_ref[rows, :]
        pair = picked[rows, :]
        theta = jnp.take_along_axis(pair, level, axis=1)
        vapour = jnp.take_along_axis(pair, level + 64, axis=1)
        supersat = vapour - 0.5 * jnp.tanh(theta)
        growth_rate = 1.0 / (1.0 + 0.1 * theta * theta)
        start = drops_ref[rows, :]
        solute = drops_ref[pl.ds(home_cap + at, BATCH), :]
        weight = drops_ref[pl.ds(2 * home_cap + at, BATCH), :]
        square = start * start
        for _ in range(SUBSTEPS):
            radius = jnp.sqrt(square)
            square = jnp.maximum(
                square
                + 0.05
                * growth_rate
                * (supersat - 0.02 / radius + solute / (radius * radius * radius)),
                0.04,
            )
        radius = jnp.sqrt(square)
        moved[rows, :] = radius
        moved[pl.ds(home_cap + at, BATCH), :] = solute
        moved[pl.ds(2 * home_cap + at, BATCH), :] = weight
        for r in range(3, 6):
            spot = drops_ref[pl.ds(r * home_cap + at, BATCH), :]
            speed = drops_ref[pl.ds((r + 3) * home_cap + at, BATCH), :]
            moved[pl.ds(r * home_cap + at, BATCH), :] = spot + 0.1 * speed
        grown = weight * (radius * square - start * start * start)
        block = at + lax.broadcasted_iota(jnp.int32, (BATCH, LANES), 0)
        mass[rows, :] = jnp.where(block < live_count, grown, 0.0)
        return carry

    lax.fori_loop(0, home_cap // BATCH, one, 0)

    def send(g, carry):
        for i in range(8):
            b = g * 8 + i
            start = (b // send_cap) * (HALF * send_cap) + b % send_cap
            block = moved[pl.ds(source_ref[b], HALF, stride=home_cap), :]
            sent_ref[pl.ds(start, HALF, stride=send_cap), :] = block
        return carry

    lax.fori_loop(0, home_cap // 8, send, 0)
    row = lax.broadcasted_iota(jnp.int32, (LANES, LANES), 0)
    column = lax.broadcasted_iota(jnp.int32, (LANES, LANES), 1)
    upper = (row <= column).astype(jnp.float32)
    mass[...] = jnp.dot(
        mass[...], upper, precision=lax.Precision.HIGHEST, preferred_element_type=jnp.float32
    )
    cond_ref[...] = jnp.zeros_like(cond_ref)
    lane = lax.broadcasted_iota(jnp.int32, (BATCH, LANES), 1)

    def sums(g, carry):
        rows = pl.ds(pl.multiple_of(g * BATCH, BATCH), BATCH)
        level = level_ref[rows, :]
        count = jnp.zeros((BATCH, LANES), jnp.int32)
        step = LANES
        while step >= 1:
            probe = jnp.minimum(count + (step - 1), LANES - 1)
            below = jnp.take_along_axis(level, probe, axis=1) <= lane
            count = jnp.where(below & (count + step <= LANES), count + step, count)
            step //= 2
        upto = jnp.take_along_axis(mass[rows, :], jnp.maximum(count - 1, 0), axis=1)
        upto = jnp.where(count > 0, upto, 0.0)
        before = jnp.where(lane == 0, 0.0, pltpu.roll(upto, 1, 1))
        picked[rows, :] = upto - before
        return carry

    lax.fori_loop(0, home_cap // BATCH, sums, 0)

    def scatter(g, carry):
        for i in range(8):
            b = g * 8 + i
            at = pl.ds(column_ref[b], 1)
            cond_ref[at, :] = cond_ref[at, :] + picked[pl.ds(b, 1), :]
        return carry

    lax.fori_loop(0, home_cap // 8, scatter, 0)


def grow_blocks(column, source, live_count, table, level, planes, send_cap):
    home_cap = level.shape[0]
    scratch = pltpu.VMEM((home_cap, LANES), jnp.float32)
    return pl.pallas_call(
        lambda *refs: grow_kernel(home_cap, send_cap, *refs),
        out_shape=(
            jax.ShapeDtypeStruct(table.shape, jnp.float32),
            jax.ShapeDtypeStruct((HALF * home_cap, LANES), jnp.float32),
        ),
        in_specs=[SMEM, SMEM, SMEM, VMEM, VMEM, VMEM],
        out_specs=(VMEM, VMEM),
        scratch_shapes=[scratch, pltpu.VMEM((HALF * home_cap, LANES), jnp.float32), scratch],
        compiler_params=params(),
        cost_estimate=cost(8 << 20, 1 << 24),
        name="grow_blocks",
    )(column, source, live_count, table, level, planes)


def place_kernel(per_device, send_cap, source_ref, arrived_ref, *refs):
    out_ref = refs[-1]

    def body(g, carry):
        for i in range(8):
            j = g * 8 + i
            source = source_ref[j]
            first = (source // send_cap) * per_device + source % send_cap
            block = arrived_ref[pl.ds(first, HALF, stride=send_cap), :]
            out_ref[pl.ds(j, HALF, stride=OWN_BLK), :] = block
        return carry

    lax.fori_loop(0, OWN_BLK // 8, body, 0)


def place_half(source, arrived, devices, send_cap, half, into):
    arrays = [source, arrived]
    specs = [SMEM, VMEM]
    aliases = {}
    if into is not None:
        arrays.append(into)
        specs.append(pl.BlockSpec(memory_space=pl.ANY))
        aliases = {2: 0}
    return pl.pallas_call(
        lambda *refs: place_kernel(arrived.shape[0] // devices, send_cap, *refs),
        grid=(1,),
        out_shape=jax.ShapeDtypeStruct((2 * HALF * OWN_BLK, LANES), jnp.float32),
        in_specs=specs,
        out_specs=pl.BlockSpec((HALF * OWN_BLK, LANES), lambda i: (half, 0)),
        input_output_aliases=aliases,
        compiler_params=params(),
        cost_estimate=cost(3 << 20, 1 << 20),
        name="place_half",
    )(*arrays)


def stencil_kernel(
    fields_ref,
    winds_ref,
    diff_ref,
    low_x,
    high_x,
    low_y,
    high_y,
    cond_ref,
    out_ref,
    ext,
    mid,
    coef,
):
    width = fields_ref.shape[1]
    merged = fields_ref.shape[2]
    lanes = merged + 2 * LANES
    core = slice(LANES, LANES + merged)
    inner = slice(ROW0, ROW0 + width)
    for k in range(9):
        if k < 5:
            own = fields_ref[k]
        elif k < 8:
            own = winds_ref[k - 5]
        else:
            own = diff_ref[...]
        ext[k, inner, core] = own
        ext[k, ROW0 - 2 : ROW0, :] = low_x[k]
        ext[k, ROW0 + width : ROW0 + width + 2, :] = high_x[k]
        ext[k, inner, 0:LANES] = low_y[k]
        ext[k, inner, LANES + merged : lanes] = high_y[k]

    chunks = range(ROW0 - 8, ROW0 + width + 8, 8)
    z = (lax.broadcasted_iota(jnp.int32, (8, lanes), 1) + (NZ - LANES % NZ)) % NZ
    top = z == NZ - 1
    bottom = z == 0

    def faces(c_low, c_high, k_low, k_high):
        courant = 0.5 * (c_low + c_high)
        diffuse = 0.5 * (k_low + k_high)
        return jnp.maximum(courant, 0.0) + diffuse, jnp.minimum(courant, 0.0) - diffuse

    def ahead(v, n):
        return pltpu.roll(v, lanes - n, 1)

    def behind(v, n):
        return pltpu.roll(v, n, 1)

    for base in chunks:
        rows = slice(base, base + 8)
        up = slice(base + 1, base + 9)
        down = slice(base - 1, base + 7)
        k0 = ext[8, rows, :]
        u0 = ext[5, rows, :]
        p, n = faces(u0, ext[5, up, :], k0, ext[8, up, :])
        p_low, n_low = faces(ext[5, down, :], u0, ext[8, down, :], k0)
        centre = 1.0 - (p - n_low)
        coef[0, rows, :] = -n
        coef[1, rows, :] = p_low
        v0 = ext[6, rows, :]
        p, n = faces(v0, ahead(v0, NZ), k0, ahead(k0, NZ))
        centre = centre - (p - behind(n, NZ))
        coef[2, rows, :] = -n
        coef[3, rows, :] = behind(p, NZ)
        w0 = ext[7, rows, :]
        p, n = faces(w0, ahead(w0, 1), k0, ahead(k0, 1))
        p = jnp.where(top, 0.0, p)
        n = jnp.where(top, 0.0, n)
        coef[4, rows, :] = -n
        p_low = jnp.where(bottom, 0.0, behind(p, 1))
        n_low = jnp.where(bottom, 0.0, behind(n, 1))
        coef[5, rows, :] = p_low
        coef[6, rows, :] = centre - (p - n_low)

    def update(src, f, base):
        rows = slice(base, base + 8)
        mine = src[f, rows, :]
        new = coef[6, rows, :] * mine
        new += coef[0, rows, :] * src[f, base + 1 : base + 9, :]
        new += coef[1, rows, :] * src[f, base - 1 : base + 7, :]
        new += coef[2, rows, :] * ahead(mine, NZ)
        new += coef[3, rows, :] * behind(mine, NZ)
        new += coef[4, rows, :] * ahead(mine, 1)
        new += coef[5, rows, :] * behind(mine, 1)
        return new

    def first(f, carry):
        for base in chunks:
            mid[f, base : base + 8, :] = update(ext, f, base)
        return carry

    lax.fori_loop(0, 5, first, 0)

    def second(f, carry):
        share = jnp.where(f == 0, 0.25, jnp.where(f == 1, -0.1, 0.0))
        for base in range(ROW0, ROW0 + width, 8):
            at = slice(base - ROW0, base - ROW0 + 8)
            out_ref[f, at, :] = update(mid, f, base)[:, core] + share * cond_ref[at, :]
        return carry

    lax.fori_loop(0, 5, second, 0)


def advance(fields, winds, diffusion, low_x, high_x, low_y, high_y, condensed):
    _, width, merged = fields.shape
    tall = ROW0 + width + 16
    wide = merged + 2 * LANES
    return pl.pallas_call(
        stencil_kernel,
        out_shape=jax.ShapeDtypeStruct(fields.shape, jnp.float32),
        in_specs=[VMEM] * 8,
        out_specs=VMEM,
        scratch_shapes=[
            pltpu.VMEM((9, tall, wide), jnp.float32),
            pltpu.VMEM((5, tall, wide), jnp.float32),
            pltpu.VMEM((7, tall, wide), jnp.float32),
        ],
        compiler_params=params(),
        cost_estimate=cost(16 << 20, 1 << 26),
        name="advance",
    )(fields, winds, diffusion, low_x, high_x, low_y, high_y, condensed)


def both_ways(low_edge, high_edge, axis):
    count = lax.axis_size(axis)
    return (
        lax.ppermute(high_edge, axis, [(i, (i + 1) % count) for i in range(count)]),
        lax.ppermute(low_edge, axis, [((i + 1) % count, i) for i in range(count)]),
    )


def per_device(fields, winds, diffusion, droplets, cells, balance_list):
    width = fields.shape[1]
    merged = fields.shape[2]
    home_cap = balance_list.shape[0]
    devices = lax.axis_size(("gx", "gy"))
    send_cap = home_cap // devices
    rows = droplets.shape[1] - 1
    column_count = width * merged // NZ

    sides = pack_sides(fields, winds, diffusion)
    sides, balance_list = lax.optimization_barrier((sides, balance_list))
    low_y, high_y = both_ways(*sides, "gy")
    live = balance_list >= 0
    owner = jnp.where(live, balance_list // OWN_BLK, devices)
    slot = balance_list % OWN_BLK
    order = lax.iota(jnp.int32, home_cap)
    earlier = (owner[:, None] == owner[None, :]) & (order[None, :] < order[:, None])
    rank = jnp.sum(earlier.astype(jnp.int32), axis=1)
    position = jnp.where(live, owner * send_cap + rank, home_cap)
    live_count = jnp.sum(live.astype(jnp.int32))[None]
    taken = position[None, :] == order[:, None]
    send_source = jnp.sum(jnp.where(taken, order[None, :], 0), axis=1)
    codes = jnp.sum(jnp.where(taken, slot[None, :] + 1, 0), axis=1) - 1
    codes = codes.astype(jnp.float32).reshape(devices, send_cap)
    codes = jnp.pad(codes, ((0, 0), (0, LANES - send_cap)))
    planes = droplets.transpose(1, 0, 2).reshape((rows + 1) * home_cap, LANES)
    everyone = ("gx", "gy")

    def exchange(x):
        return lax.all_to_all(x, everyone, split_axis=0, concat_axis=0, tiled=True)

    outgoing = send_rows(send_source, codes, planes, home_cap, send_cap)
    outgoing, low_y, high_y, fields, winds, diffusion, cells = lax.optimization_barrier(
        (outgoing, low_y, high_y, fields, winds, diffusion, cells)
    )
    arrived = exchange(outgoing)

    def edge(xs):
        grids = (fields, winds, diffusion[None])
        own = jnp.concatenate([g[:, xs] for g in grids], axis=0)
        return jnp.concatenate([low_y[:, xs], own, high_y[:, xs]], axis=2)

    x_edges = (edge(slice(0, 2)), edge(slice(width - 2, width)))
    x_edges, cells, fields = lax.optimization_barrier((x_edges, cells, fields))
    column = cells[:, 0] // NZ
    low_x, high_x = both_ways(*x_edges, "gx")

    level = cells % NZ
    gap = jnp.zeros((column_count, LANES // 2 - NZ), jnp.float32)
    table = jnp.concatenate(
        [
            fields[0].reshape(column_count, NZ),
            gap,
            fields[1].reshape(column_count, NZ),
            gap,
        ],
        axis=1,
    )
    condensed, second = grow_blocks(
        column, send_source, live_count, table, level, planes, send_cap
    )
    second, low_x, high_x = lax.optimization_barrier((second, low_x, high_x))
    arrived, low_x, high_x = lax.optimization_barrier((arrived, low_x, high_x))
    arrived_second = exchange(second)
    condensed = condensed[:, :NZ].reshape(width, merged)
    fields_out = advance(fields, winds, diffusion, low_x, high_x, low_y, high_y, condensed)

    per_device_rows = arrived.shape[0] // devices
    arrived_codes = arrived.reshape(devices, per_device_rows, LANES)[
        :, HALF * send_cap, :send_cap
    ].reshape(-1)
    own = lax.iota(jnp.int32, OWN_BLK).astype(jnp.float32)
    source = jnp.sum(
        jnp.where(arrived_codes[None, :] == own[:, None], order[None, :], 0), axis=1
    )
    placed = place_half(source, arrived, devices, send_cap, 1, None)
    placed, fields_out = lax.optimization_barrier((placed, fields_out))
    placed = place_half(source, arrived_second, devices, send_cap, 0, placed)
    droplets_out = placed.reshape(2 * HALF, OWN_BLK, LANES).transpose(1, 0, 2)
    return (fields_out, droplets_out)


def solution(mesh):
    return jax.shard_map(
        per_device,
        mesh=mesh,
        in_specs=(
            P(None, "gx", "gy"),
            P(None, "gx", "gy"),
            P("gx", "gy"),
            P(("gx", "gy"), None, None),
            P(("gx", "gy"), None),
            P(("gx", "gy")),
        ),
        out_specs=(P(None, "gx", "gy"), P(("gx", "gy"), None, None)),
        check_vma=False,
    )
```

```python
import jax
import jax.numpy as jnp
from jax import lax
from jax.experimental import pallas as pl
from jax.experimental.pallas import tpu as pltpu
from jax.sharding import PartitionSpec as P

NZ = 48
OWN_BLK = 256
SUBSTEPS = 4
LANES = 128
ROW0 = 16
BATCH = 64
VMEM = pl.BlockSpec(memory_space=pltpu.VMEM)
SMEM = pl.BlockSpec(memory_space=pltpu.SMEM)
LIMIT = 56 * 1024 * 1024


def params():
    return pltpu.CompilerParams(vmem_limit_bytes=LIMIT)


def cost(bytes_accessed, flops):
    return pl.CostEstimate(flops=flops, bytes_accessed=bytes_accessed, transcendentals=0)


CODE_ROWS = 8


def pack_kernel(f_low, f_high, w_low, w_high, d_low, d_high, low_ref, high_ref):
    for f, w, d, out in ((f_low, w_low, d_low, low_ref), (f_high, w_high, d_high, high_ref)):
        out[0:5] = f[...]
        out[5:8] = w[...]
        out[8] = d[...]


def pack_sides(fields, winds, diffusion):
    _, width, merged = fields.shape
    last = merged // LANES - 1
    specs = []
    for count in (5, 3):
        for at in (0, last):
            specs.append(pl.BlockSpec((count, width, LANES), lambda i, at=at: (0, 0, at)))
    for at in (0, last):
        specs.append(pl.BlockSpec((width, LANES), lambda i, at=at: (0, at)))
    shape = jax.ShapeDtypeStruct((9, width, LANES), jnp.float32)
    whole = pl.BlockSpec((9, width, LANES), lambda i: (0, 0, 0))
    return pl.pallas_call(
        pack_kernel,
        grid=(1,),
        out_shape=(shape, shape),
        in_specs=specs,
        out_specs=(whole, whole),
        cost_estimate=cost(1 << 20, 1 << 10),
        name="pack_sides",
    )(fields, fields, winds, winds, diffusion, diffusion)


def send_kernel(home_cap, send_cap, rows, steps, source_ref, code_ref, drops_ref, out_ref):
    devices = home_cap // send_cap // steps
    per_device = rows * send_cap + CODE_ROWS
    first = pl.program_id(0) * devices

    def body(d, carry):
        start = d * per_device
        for i in range(send_cap):
            b = source_ref[(first + d) * send_cap + i]
            block = drops_ref[pl.ds(home_cap + b, rows, stride=home_cap), :]
            out_ref[pl.ds(start + i, rows, stride=send_cap), :] = block
        out_ref[pl.ds(start + rows * send_cap, 1), :] = code_ref[pl.ds(first + d, 1), :]
        return carry

    lax.fori_loop(0, devices, body, 0)


def send_rows(source, codes, planes, home_cap, send_cap):
    rows = planes.shape[0] // home_cap - 1
    devices = home_cap // send_cap
    total = devices * (rows * send_cap + CODE_ROWS)
    steps = 4
    return pl.pallas_call(
        lambda *refs: send_kernel(home_cap, send_cap, rows, steps, *refs),
        grid=(steps,),
        out_shape=jax.ShapeDtypeStruct((total, LANES), jnp.float32),
        in_specs=[SMEM, VMEM, VMEM],
        out_specs=pl.BlockSpec((total // steps, LANES), lambda i: (i, 0)),
        compiler_params=params(),
        cost_estimate=cost(6 << 20, 1 << 20),
        name="send_rows",
    )(source, codes, planes)


def grow_kernel(
    home_cap,
    column_ref,
    source_ref,
    live_ref,
    table_ref,
    level_ref,
    drops_ref,
    cond_ref,
    sent_ref,
    picked,
    radius_out,
    mass,
):
    live_count = live_ref[0]

    def fetch(g, carry):
        for i in range(8):
            b = g * 8 + i
            picked[pl.ds(b, 1), :] = table_ref[pl.ds(column_ref[b], 1), :]
        return carry

    lax.fori_loop(0, home_cap // 8, fetch, 0)

    def one(g, carry):
        at = pl.multiple_of(g * BATCH, BATCH)
        rows = pl.ds(at, BATCH)
        level = level_ref[rows, :]
        pair = picked[rows, :]
        theta = jnp.take_along_axis(pair, level, axis=1)
        vapour = jnp.take_along_axis(pair, level + 64, axis=1)
        supersat = vapour - 0.5 * jnp.tanh(theta)
        growth_rate = 1.0 / (1.0 + 0.1 * theta * theta)
        start = drops_ref[rows, :]
        solute = drops_ref[pl.ds(home_cap + at, BATCH), :]
        weight = drops_ref[pl.ds(2 * home_cap + at, BATCH), :]
        square = start * start
        for _ in range(SUBSTEPS):
            radius = jnp.sqrt(square)
            square = jnp.maximum(
                square
                + 0.05
                * growth_rate
                * (supersat - 0.02 / radius + solute / (radius * radius * radius)),
                0.04,
            )
        radius = jnp.sqrt(square)
        radius_out[rows, :] = radius
        grown = weight * (radius * square - start * start * start)
        block = at + lax.broadcasted_iota(jnp.int32, (BATCH, LANES), 0)
        mass[rows, :] = jnp.where(block < live_count, grown, 0.0)
        return carry

    lax.fori_loop(0, home_cap // BATCH, one, 0)

    def send(g, carry):
        for i in range(8):
            b = g * 8 + i
            sent_ref[pl.ds(b, 1), :] = radius_out[pl.ds(source_ref[b], 1), :]
        return carry

    lax.fori_loop(0, home_cap // 8, send, 0)
    row = lax.broadcasted_iota(jnp.int32, (LANES, LANES), 0)
    column = lax.broadcasted_iota(jnp.int32, (LANES, LANES), 1)
    upper = (row <= column).astype(jnp.float32)
    mass[...] = jnp.dot(
        mass[...], upper, precision=lax.Precision.HIGHEST, preferred_element_type=jnp.float32
    )
    cond_ref[...] = jnp.zeros_like(cond_ref)
    lane = lax.broadcasted_iota(jnp.int32, (BATCH, LANES), 1)

    def sums(g, carry):
        rows = pl.ds(pl.multiple_of(g * BATCH, BATCH), BATCH)
        level = level_ref[rows, :]
        count = jnp.zeros((BATCH, LANES), jnp.int32)
        step = LANES
        while step >= 1:
            probe = jnp.minimum(count + (step - 1), LANES - 1)
            below = jnp.take_along_axis(level, probe, axis=1) <= lane
            count = jnp.where(below & (count + step <= LANES), count + step, count)
            step //= 2
        upto = jnp.take_along_axis(mass[rows, :], jnp.maximum(count - 1, 0), axis=1)
        upto = jnp.where(count > 0, upto, 0.0)
        before = jnp.where(lane == 0, 0.0, pltpu.roll(upto, 1, 1))
        picked[rows, :] = upto - before
        return carry

    lax.fori_loop(0, home_cap // BATCH, sums, 0)

    def scatter(g, carry):
        for i in range(8):
            b = g * 8 + i
            at = pl.ds(column_ref[b], 1)
            cond_ref[at, :] = cond_ref[at, :] + picked[pl.ds(b, 1), :]
        return carry

    lax.fori_loop(0, home_cap // 8, scatter, 0)


def grow_blocks(column, source, live_count, table, level, planes):
    home_cap = level.shape[0]
    scratch = pltpu.VMEM((home_cap, LANES), jnp.float32)
    return pl.pallas_call(
        lambda *refs: grow_kernel(home_cap, *refs),
        out_shape=(
            jax.ShapeDtypeStruct(table.shape, jnp.float32),
            jax.ShapeDtypeStruct((home_cap, LANES), jnp.float32),
        ),
        in_specs=[SMEM, SMEM, SMEM, VMEM, VMEM, VMEM],
        out_specs=(VMEM, VMEM),
        scratch_shapes=[scratch, scratch, scratch],
        compiler_params=params(),
        cost_estimate=cost(8 << 20, 1 << 24),
        name="grow_blocks",
    )(column, source, live_count, table, level, planes)


def place_kernel(home_cap, send_cap, rows, source_ref, arrived_ref, out_ref):
    per_device = rows * send_cap + CODE_ROWS

    def body(g, carry):
        for i in range(8):
            j = g * 8 + i
            source = source_ref[j]
            first = (source // send_cap) * per_device + source % send_cap
            block = arrived_ref[pl.ds(first, rows, stride=send_cap), :]
            out_ref[pl.ds(OWN_BLK + j, rows, stride=OWN_BLK), :] = block
        return carry

    lax.fori_loop(0, OWN_BLK // 8, body, 0)
    for r in range(3, 6):
        at = pl.ds(r * OWN_BLK, OWN_BLK)
        out_ref[at, :] = out_ref[at, :] + 0.1 * out_ref[pl.ds((r + 3) * OWN_BLK, OWN_BLK), :]


def place_blocks(source, arrived, home_cap, send_cap, rows):
    return pl.pallas_call(
        lambda *refs: place_kernel(home_cap, send_cap, rows, *refs),
        out_shape=jax.ShapeDtypeStruct(((rows + 1) * OWN_BLK, LANES), jnp.float32),
        in_specs=[SMEM, VMEM],
        out_specs=VMEM,
        compiler_params=params(),
        cost_estimate=cost(5 << 20, 1 << 20),
        name="place_blocks",
    )(source, arrived)


def place_radius_kernel(source_ref, radius_ref, placed_ref, out_ref, rows_ref, sem):
    def body(g, carry):
        for i in range(8):
            j = g * 8 + i
            rows_ref[pl.ds(j, 1), :] = radius_ref[pl.ds(source_ref[j], 1), :]
        return carry

    lax.fori_loop(0, OWN_BLK // 8, body, 0)
    copy = pltpu.make_async_copy(rows_ref, out_ref.at[pl.ds(0, OWN_BLK), :], sem)
    copy.start()
    copy.wait()


def place_radius(source, radius, placed):
    return pl.pallas_call(
        place_radius_kernel,
        out_shape=jax.ShapeDtypeStruct(placed.shape, jnp.float32),
        in_specs=[SMEM, VMEM, pl.BlockSpec(memory_space=pl.ANY)],
        out_specs=pl.BlockSpec(memory_space=pl.ANY),
        scratch_shapes=[pltpu.VMEM((OWN_BLK, LANES), jnp.float32), pltpu.SemaphoreType.DMA],
        input_output_aliases={2: 0},
        compiler_params=params(),
        cost_estimate=cost(1 << 19, 1 << 16),
        name="place_radius",
    )(source, radius, placed)


def stencil_kernel(
    fields_ref,
    winds_ref,
    diff_ref,
    low_x,
    high_x,
    low_y,
    high_y,
    cond_ref,
    out_ref,
    ext,
    mid,
    coef,
):
    width = fields_ref.shape[1]
    merged = fields_ref.shape[2]
    lanes = merged + 2 * LANES
    core = slice(LANES, LANES + merged)
    inner = slice(ROW0, ROW0 + width)
    for k in range(9):
        if k < 5:
            own = fields_ref[k]
        elif k < 8:
            own = winds_ref[k - 5]
        else:
            own = diff_ref[...]
        ext[k, inner, core] = own
        ext[k, ROW0 - 2 : ROW0, :] = low_x[k]
        ext[k, ROW0 + width : ROW0 + width + 2, :] = high_x[k]
        ext[k, inner, 0:LANES] = low_y[k]
        ext[k, inner, LANES + merged : lanes] = high_y[k]

    chunks = range(ROW0 - 8, ROW0 + width + 8, 8)
    z = (lax.broadcasted_iota(jnp.int32, (8, lanes), 1) + (NZ - LANES % NZ)) % NZ
    top = z == NZ - 1
    bottom = z == 0

    def faces(c_low, c_high, k_low, k_high):
        courant = 0.5 * (c_low + c_high)
        diffuse = 0.5 * (k_low + k_high)
        return jnp.maximum(courant, 0.0) + diffuse, jnp.minimum(courant, 0.0) - diffuse

    def ahead(v, n):
        return pltpu.roll(v, lanes - n, 1)

    def behind(v, n):
        return pltpu.roll(v, n, 1)

    for base in chunks:
        rows = slice(base, base + 8)
        up = slice(base + 1, base + 9)
        down = slice(base - 1, base + 7)
        k0 = ext[8, rows, :]
        u0 = ext[5, rows, :]
        p, n = faces(u0, ext[5, up, :], k0, ext[8, up, :])
        p_low, n_low = faces(ext[5, down, :], u0, ext[8, down, :], k0)
        centre = 1.0 - (p - n_low)
        coef[0, rows, :] = -n
        coef[1, rows, :] = p_low
        v0 = ext[6, rows, :]
        p, n = faces(v0, ahead(v0, NZ), k0, ahead(k0, NZ))
        centre = centre - (p - behind(n, NZ))
        coef[2, rows, :] = -n
        coef[3, rows, :] = behind(p, NZ)
        w0 = ext[7, rows, :]
        p, n = faces(w0, ahead(w0, 1), k0, ahead(k0, 1))
        p = jnp.where(top, 0.0, p)
        n = jnp.where(top, 0.0, n)
        coef[4, rows, :] = -n
        p_low = jnp.where(bottom, 0.0, behind(p, 1))
        n_low = jnp.where(bottom, 0.0, behind(n, 1))
        coef[5, rows, :] = p_low
        coef[6, rows, :] = centre - (p - n_low)

    def update(src, f, base):
        rows = slice(base, base + 8)
        mine = src[f, rows, :]
        new = coef[6, rows, :] * mine
        new += coef[0, rows, :] * src[f, base + 1 : base + 9, :]
        new += coef[1, rows, :] * src[f, base - 1 : base + 7, :]
        new += coef[2, rows, :] * ahead(mine, NZ)
        new += coef[3, rows, :] * behind(mine, NZ)
        new += coef[4, rows, :] * ahead(mine, 1)
        new += coef[5, rows, :] * behind(mine, 1)
        return new

    def first(f, carry):
        for base in chunks:
            mid[f, base : base + 8, :] = update(ext, f, base)
        return carry

    lax.fori_loop(0, 5, first, 0)

    def second(f, carry):
        share = jnp.where(f == 0, 0.25, jnp.where(f == 1, -0.1, 0.0))
        for base in range(ROW0, ROW0 + width, 8):
            at = slice(base - ROW0, base - ROW0 + 8)
            out_ref[f, at, :] = update(mid, f, base)[:, core] + share * cond_ref[at, :]
        return carry

    lax.fori_loop(0, 5, second, 0)


def advance(fields, winds, diffusion, low_x, high_x, low_y, high_y, condensed):
    _, width, merged = fields.shape
    tall = ROW0 + width + 16
    wide = merged + 2 * LANES
    return pl.pallas_call(
        stencil_kernel,
        out_shape=jax.ShapeDtypeStruct(fields.shape, jnp.float32),
        in_specs=[VMEM] * 8,
        out_specs=VMEM,
        scratch_shapes=[
            pltpu.VMEM((9, tall, wide), jnp.float32),
            pltpu.VMEM((5, tall, wide), jnp.float32),
            pltpu.VMEM((7, tall, wide), jnp.float32),
        ],
        compiler_params=params(),
        cost_estimate=cost(16 << 20, 1 << 26),
        name="advance",
    )(fields, winds, diffusion, low_x, high_x, low_y, high_y, condensed)


def both_ways(low_edge, high_edge, axis):
    count = lax.axis_size(axis)
    return (
        lax.ppermute(high_edge, axis, [(i, (i + 1) % count) for i in range(count)]),
        lax.ppermute(low_edge, axis, [((i + 1) % count, i) for i in range(count)]),
    )


def per_device(fields, winds, diffusion, droplets, cells, balance_list):
    width = fields.shape[1]
    merged = fields.shape[2]
    home_cap = balance_list.shape[0]
    devices = lax.axis_size(("gx", "gy"))
    send_cap = home_cap // devices
    rows = droplets.shape[1] - 1
    column_count = width * merged // NZ

    sides = pack_sides(fields, winds, diffusion)
    sides, balance_list = lax.optimization_barrier((sides, balance_list))
    low_y, high_y = both_ways(*sides, "gy")
    live = balance_list >= 0
    owner = jnp.where(live, balance_list // OWN_BLK, devices)
    slot = balance_list % OWN_BLK
    order = lax.iota(jnp.int32, home_cap)
    earlier = (owner[:, None] == owner[None, :]) & (order[None, :] < order[:, None])
    rank = jnp.sum(earlier.astype(jnp.int32), axis=1)
    position = jnp.where(live, owner * send_cap + rank, home_cap)
    live_count = jnp.sum(live.astype(jnp.int32))[None]
    taken = position[None, :] == order[:, None]
    send_source = jnp.sum(jnp.where(taken, order[None, :], 0), axis=1)
    codes = jnp.sum(jnp.where(taken, slot[None, :] + 1, 0), axis=1) - 1
    codes = codes.astype(jnp.float32).reshape(devices, send_cap)
    codes = jnp.pad(codes, ((0, 0), (0, LANES - send_cap)))
    planes = droplets.transpose(1, 0, 2).reshape((rows + 1) * home_cap, LANES)
    everyone = ("gx", "gy")

    def exchange(x):
        return lax.all_to_all(x, everyone, split_axis=0, concat_axis=0, tiled=True)

    outgoing = send_rows(send_source, codes, planes, home_cap, send_cap)
    outgoing, low_y, high_y, fields, winds, diffusion, cells = lax.optimization_barrier(
        (outgoing, low_y, high_y, fields, winds, diffusion, cells)
    )
    arrived = exchange(outgoing)

    def edge(xs):
        grids = (fields, winds, diffusion[None])
        own = jnp.concatenate([g[:, xs] for g in grids], axis=0)
        return jnp.concatenate([low_y[:, xs], own, high_y[:, xs]], axis=2)

    x_edges = (edge(slice(0, 2)), edge(slice(width - 2, width)))
    x_edges, cells, fields = lax.optimization_barrier((x_edges, cells, fields))
    column = cells[:, 0] // NZ
    low_x, high_x = both_ways(*x_edges, "gx")

    level = cells % NZ
    gap = jnp.zeros((column_count, LANES // 2 - NZ), jnp.float32)
    table = jnp.concatenate(
        [
            fields[0].reshape(column_count, NZ),
            gap,
            fields[1].reshape(column_count, NZ),
            gap,
        ],
        axis=1,
    )
    condensed, radius = grow_blocks(column, send_source, live_count, table, level, planes)
    condensed = condensed[:, :NZ].reshape(width, merged)
    fields_out = advance(fields, winds, diffusion, low_x, high_x, low_y, high_y, condensed)

    arrived, radius, fields_out = lax.optimization_barrier((arrived, radius, fields_out))
    arrived_radius = exchange(radius)
    per_device_rows = arrived.shape[0] // devices
    arrived_codes = arrived.reshape(devices, per_device_rows, LANES)[
        :, rows * send_cap, :send_cap
    ].reshape(-1)
    own = lax.iota(jnp.int32, OWN_BLK).astype(jnp.float32)
    source = jnp.sum(
        jnp.where(arrived_codes[None, :] == own[:, None], order[None, :], 0), axis=1
    )
    placed = place_blocks(source, arrived, home_cap, send_cap, rows)
    placed = place_radius(source, arrived_radius, placed)
    droplets_out = placed.reshape(rows + 1, OWN_BLK, LANES).transpose(1, 0, 2)
    return (fields_out, droplets_out)


def solution(mesh):
    return jax.shard_map(
        per_device,
        mesh=mesh,
        in_specs=(
            P(None, "gx", "gy"),
            P(None, "gx", "gy"),
            P("gx", "gy"),
            P(("gx", "gy"), None, None),
            P(("gx", "gy"), None),
            P(("gx", "gy")),
        ),
        out_specs=(P(None, "gx", "gy"), P(("gx", "gy"), None, None)),
        check_vma=False,
    )
```
